32 devices in a mesh: grp: 2 (over y), seq: 16 (over z, x, core).
Axes of the slice: x: 2, y: 2, z: 4, core: 2. Of those that a mesh axis runs over, the one named last changes fastest.
Arguments:
- query: bfloat16 [4096, 2560], P(('grp', 'seq')), parts along dimension 0, may hold values from -6 to 6
- key: bfloat16 [4096, 2560], P(('grp', 'seq')), parts along dimension 0, may hold values from -6 to 6
- value: bfloat16 [4096, 2560], P(('grp', 'seq')), parts along dimension 0, may hold values from -6 to 6
- grad_out: bfloat16 [4096, 2560], P(('grp', 'seq')), parts along dimension 0, may hold values from -6 to 6
- tile_mask: int32 [16, 7, 1, 1], P('seq'), may hold values from 0 to 1, as said below
Outputs:
- attended: bfloat16 [4096, 2560], P(('grp', 'seq')), parts along dimension 0
- grad_query: bfloat16 [4096, 2560], P(('grp', 'seq')), parts along dimension 0
- grad_key: bfloat16 [4096, 2560], P(('grp', 'seq')), parts along dimension 0
- grad_value: bfloat16 [4096, 2560], P(('grp', 'seq')), parts along dimension 0
The draws below stay inside these ranges and needn't reach their ends.
There are 2 independent parts, one for each index of `grp`. The reference program is written for one: setup_inputs(seed, part) draws one part's arguments, and reference() takes and returns one part's arrays. A program takes and returns all parts, laid end to end along the dimension named above; an argument that names none is the same for every part. Nothing has to cross between parts.
Inputs may be any that keep to these rules, and one draw needn't show every extreme that they name: tile_mask[i, d, a, b] allows query tile a of shard i to attend to key tile b of shard i + o_d, with o_0 = 0, o_(2k+1) = 2**k, o_(2k+2) = -2**k; offset 0 is all ones; entries toward shards outside the sequence are 0.
All inputs are finite; a program needn't handle non-finite values.
Results may differ from the reference program's by a relative error of at most 0.019.
Values may be sent and summed in bfloat16 or wider, within the bound.
A program may use at most 128 MiB of HBM per device.

```python
import jax
import jax.numpy as jnp
from jax import lax

HEADS = 20
HEAD = 128
TILE = 128
LEVELS = 3
ROWS_DEV = 128
HD = 2560
DISTS = 7
TB = 1
TOKENS = 2048
N_SEQ = 16


def base_rows(key):
    return jnp.clip(jax.random.normal(key, (TOKENS, HEADS * HEAD), jnp.float32), -6.0, 6.0)


def draw_query(key, part):
    values = base_rows(jax.random.fold_in(key, 21))
    return values.astype(jnp.bfloat16)


def draw_key(key, part):
    values = base_rows(jax.random.fold_in(key, 22))
    return values.astype(jnp.bfloat16)


def draw_tile_mask(key, part):
    offsets = jnp.array([0] + [direction * 2 ** level_index for level_index in range(LEVELS) for direction in (1, -1)], jnp.int32)
    divisor = jnp.array([1] + [level_index + 2 for level_index in range(LEVELS) for direction in (1, -1)], jnp.int32)
    ticket = jax.random.randint(jax.random.fold_in(key, 11), (N_SEQ, DISTS, TB, TB), 0, 60)
    keeping = ticket % divisor[None, :, None, None] == 0
    partner = jnp.arange(N_SEQ, dtype=jnp.int32)[:, None] + offsets[None, :]
    inside = (partner >= 0) & (partner < N_SEQ)
    return (keeping & inside[:, :, None, None]).astype(jnp.int32)


def block_levels(key, dims, pieces, least, largest):
    level, own = 1.0, jax.random.fold_in(key, 6)
    for position, parts in pieces:
        heights = jnp.exp(jax.random.uniform(jax.random.fold_in(own, position), (parts,), jnp.float32, least / len(pieces), largest / len(pieces)))
        level = level * jnp.repeat(heights, dims[position] // parts).reshape([-1 if axis == position else 1 for axis in range(len(dims))])
    return level


def centred(own_key, extent, deviation, bound, shards=(), kind=jnp.bfloat16):
    factor_of = block_levels(own_key, extent, shards, -0.22, 0.18) if shards else 1.0
    values = jax.random.normal(own_key, extent, jnp.float32) * deviation * factor_of
    return jnp.minimum(jnp.maximum(values, -bound), bound).astype(kind)


def setup_inputs(seed: int = 0, part: int = 0) -> dict:
    key_list = jax.random.split(jax.random.key(seed), 6)
    part_splits = jax.random.split(jax.random.fold_in(key_list[5], part), 6)
    query = draw_query(jax.random.fold_in(jax.random.fold_in(key_list[5], part), 71), part)
    key = draw_key(jax.random.fold_in(jax.random.fold_in(key_list[5], part), 71), part)
    value = centred(part_splits[2], (TOKENS, HD), 1.0, 6.0, ((0, 16),))
    grad_out = centred(part_splits[3], (TOKENS, HD), 1.0, 6.0, ((0, 16),))
    tile_mask = draw_tile_mask(jax.random.fold_in(key_list[5], 71), part)
    return dict(query=query, key=key, value=value, grad_out=grad_out, tile_mask=tile_mask)


NEG = -1.0e30


def offset_list(level_total):
    return [0] + [direction * 2 ** level_index for level_index in range(level_total) for direction in (1, -1)]


def shift_rows(array, offset):
    shard_total = array.shape[0]
    if offset == 0:
        return array
    padding = jnp.zeros((abs(offset),) + array.shape[1:], array.dtype)
    if offset > 0:
        return jnp.concatenate([array[offset:], padding], 0)
    return jnp.concatenate([padding, array[:shard_total + offset]], 0)


def narrow(array):
    return lax.optimization_barrier(array.astype(jnp.bfloat16)).astype(jnp.float32)


def expand(tile_mask, dist_index):
    flags = tile_mask[:, dist_index]
    full_mask = jnp.broadcast_to(flags[:, :, None, :, None], (N_SEQ, TB, TILE, TB, TILE)).reshape(N_SEQ, ROWS_DEV, ROWS_DEV)
    return (full_mask > 0)[:, None]


def reference(query, key, value, grad_out, tile_mask):
    shape4 = (N_SEQ, ROWS_DEV, HEADS, HEAD)
    query_f = query.reshape(shape4).astype(jnp.float32)
    key_f = key.reshape(shape4).astype(jnp.float32)
    value_f = value.reshape(shape4).astype(jnp.float32)
    grad_f = grad_out.reshape(shape4).astype(jnp.float32)
    score_scale = HEAD ** -0.5
    offsets = offset_list(LEVELS)

    def masked_scores(dist_index, offset):
        remote = shift_rows(key_f, offset)
        scores = jnp.einsum("nqhd,nkhd->nhqk", query_f, remote) * score_scale
        allowed = expand(tile_mask, dist_index)
        return allowed, jnp.where(allowed, scores, NEG)

    top = jnp.full((N_SEQ, HEADS, ROWS_DEV), NEG, jnp.float32)
    total = jnp.zeros((N_SEQ, HEADS, ROWS_DEV), jnp.float32)
    for dist_index, offset in enumerate(offsets):
        allowed, scores = masked_scores(dist_index, offset)
        newtop = jnp.maximum(top, jnp.max(scores, -1))
        total = total * jnp.exp(top - newtop) + jnp.sum(jnp.exp(scores - newtop[..., None]), -1)
        top = newtop
    log_total = top + jnp.log(total)

    out_acc = jnp.zeros(shape4, jnp.float32)
    for dist_index, offset in enumerate(offsets):
        allowed, scores = masked_scores(dist_index, offset)
        probs = narrow(jnp.where(allowed, jnp.exp(scores - log_total[..., None]), 0.0))
        out_acc = out_acc + jnp.einsum("nhqk,nkhd->nqhd", probs, shift_rows(value_f, offset))
    attended = out_acc.astype(jnp.bfloat16)

    delta = jnp.sum(grad_f * attended.astype(jnp.float32), -1)
    delta = jnp.transpose(delta, (0, 2, 1))
    query_acc = jnp.zeros(shape4, jnp.float32)
    key_acc = jnp.zeros(shape4, jnp.float32)
    value_acc = jnp.zeros(shape4, jnp.float32)
    for dist_index, offset in enumerate(offsets):
        allowed, scores = masked_scores(dist_index, offset)
        exact = jnp.where(allowed, jnp.exp(scores - log_total[..., None]), 0.0)
        probs = narrow(exact)
        remote_keys = shift_rows(key_f, offset)
        remote_values = shift_rows(value_f, offset)
        dprobs = jnp.einsum("nqhd,nkhd->nhqk", grad_f, remote_values)
        dscores = narrow(exact * (dprobs - delta[..., None]))
        query_acc = query_acc + jnp.einsum("nhqk,nkhd->nqhd", dscores, remote_keys)
        key_part = jnp.einsum("nhqk,nqhd->nkhd", dscores, query_f) * score_scale
        value_part = jnp.einsum("nhqk,nqhd->nkhd", probs, grad_f)
        if offset != 0:
            key_part = narrow(key_part)
            value_part = narrow(value_part)
        key_acc = key_acc + shift_rows(key_part, -offset)
        value_acc = value_acc + shift_rows(value_part, -offset)
    flat = (N_SEQ * ROWS_DEV, HEADS * HEAD)
    grad_query = (query_acc * score_scale).reshape(flat).astype(jnp.bfloat16)
    grad_key = key_acc.reshape(flat).astype(jnp.bfloat16)
    grad_value = value_acc.reshape(flat).astype(jnp.bfloat16)
    return (attended.reshape(flat), grad_query, grad_key, grad_value)
```

```python
import functools

import jax
import jax.numpy as jnp
from jax import lax
from jax.experimental import pallas as pl
from jax.experimental.pallas import tpu as pltpu
from jax.sharding import PartitionSpec as P

HEAD = 128
ROW = 4
BIG = 1e30
DIST = {0: 0, 1: 1, -1: 2, 2: 3, -2: 4, 4: 5, -4: 6}

OWN, UP, DN = range(3)
KV, QG = range(2)
OUT, GQ, GK, GV = range(4)
SHIFT = {OWN: 0, UP: ROW, DN: -ROW}
NT = (((1,), (1,)), ((), ()))


def readers(a, sign):
    found = []
    for side in (OWN, UP, DN):
        for b in range(ROW):
            offset = sign * (SHIFT[side] + b - a)
            if offset in DIST:
                found.append((side, b, DIST[offset]))
    return found


def kernel(seq, mask_ref, q_ref, k_ref, v_ref, g_ref, out_ref,
           rb, held, bias, stats,
           load_sem, row_send, row_recv, z_send, z_recv, bias_send, bias_recv, zbias_send, zbias_recv,
           stat_send, stat_recv, own_sem, ret_send, ret_recv):
    rows = q_ref.shape[0]
    heads = q_ref.shape[1] // HEAD // ROW
    scale = HEAD ** (-0.5)
    sources = ((k_ref, v_ref), (q_ref, g_ref))

    me = lax.axis_index("seq")
    place = lax.rem(me, ROW)
    first = me - place
    core = lax.rem(place, 2)
    sib = place + 1 - 2 * core
    mates = {1: sib, 2: lax.rem(place + 2, ROW), 3: lax.rem(sib + 2, ROW)}
    shard_of = {0: place, **mates}
    exists = {UP: me + ROW < seq, DN: me >= ROW}
    target = {UP: me + ROW, DN: me - ROW}
    other = {UP: DN, DN: UP}

    def remote(src, dst, send, recv, device):
        return pltpu.make_async_remote_copy(
            src_ref=src, dst_ref=dst, send_sem=send, recv_sem=recv,
            device_id={"seq": device}, device_id_type=pl.DeviceIdType.MESH,
        )

    def columns(part, h):
        return pl.ds(pl.multiple_of((part * heads + h) * HEAD, HEAD), HEAD)

    barrier = pltpu.get_barrier_semaphore()
    for m in (1, 2, 3):
        pl.semaphore_signal(barrier, inc=1, device_id={"seq": first + mates[m]})
    for side in (UP, DN):
        @pl.when(exists[side])
        def _(side=side):
            pl.semaphore_signal(barrier, inc=1, device_id={"seq": target[side]})

    def load(h, carry):
        for t in (KV, QG):
            for j in range(2):
                pltpu.make_async_copy(
                    sources[t][j].at[:, columns(place, h)], rb.at[OWN, t, h, place, j], load_sem.at[t, h]
                ).start()
        return carry

    lax.fori_loop(0, heads, load, 0)

    index = lax.broadcasted_iota(jnp.int32, (8, 128), 0)
    tile = jnp.zeros((8, 128), jnp.float32)
    for d in range(7):
        tile = jnp.where(index == d, (1.0 - mask_ref[d].astype(jnp.float32)) * BIG, tile)
    bias[OWN, place] = tile

    def row_copy(m, t, h, j):
        return remote(
            sources[t][j].at[:, columns(mates[m], h)], rb.at[OWN, t, h, place, j],
            row_send.at[t, h, m - 1], row_recv.at[t, h, m - 1], first + mates[m],
        )

    def row_pair(m, t, h):
        pair = rb.at[OWN, t, h, shard_of[m]]
        return remote(pair, pair, row_send.at[t, h, m - 1], row_recv.at[t, h, m - 1], first + mates[m])

    def bias_copy(m, shard):
        return remote(
            bias.at[OWN, shard], bias.at[OWN, shard], bias_send.at[m - 1], bias_recv.at[m - 1], first + mates[m]
        )

    def zbias_copy(side, landing):
        return remote(bias.at[OWN], bias.at[landing], zbias_send.at[side], zbias_recv.at[landing], target[side])

    def z_copy(side, t, h, shard):
        return remote(
            rb.at[OWN, t, h, shard], rb.at[other[side], t, h, shard],
            z_send.at[side, t, h], z_recv.at[other[side], t, h], target[side],
        )

    def z_whole(side, t, h):
        return remote(
            rb.at[OWN, t, h], rb.at[side, t, h], z_send.at[side, t, h], z_recv.at[side, t, h], target[side]
        )

    def stat_copy(side, landing, h):
        return remote(
            stats.at[OWN, h], stats.at[landing, h], stat_send.at[side, h], stat_recv.at[landing, h], target[side]
        )

    def own_copy(j, h):
        return pltpu.make_async_copy(
            held.at[j, h, place], out_ref.at[j, :, columns(place, h)], own_sem.at[j, h]
        )

    def return_copy(m, j, h):
        return remote(
            held.at[j, h, mates[m]], out_ref.at[j, :, columns(place, h)],
            ret_send.at[j, h], ret_recv.at[m - 1], first + mates[m],
        )

    def exchange(t, h):
        for m in (2, 3, 1):
            for j in range(2):
                row_copy(m, t, h, j).start()

    def forward(m, t, h):
        if m == 0:
            pair = rb.at[OWN, t, h, place]
            pltpu.make_async_copy(pair, pair, load_sem.at[t, h]).wait()
        else:
            row_pair(m, t, h).wait_recv()
        for side in (UP, DN):
            @pl.when(exists[side])
            def _(side=side):
                z_copy(side, t, h, shard_of[m]).start()

    def z_arrived(t, h):
        for side in (UP, DN):
            @pl.when(exists[side])
            def _(side=side):
                z_whole(side, t, h).wait_recv()

    def give_back(j, h):
        for m in (2, 3, 1):
            return_copy(m, j, h).start()
        own_copy(j, h).start()

    def stacked(t, h, j, places):
        return jnp.concatenate([rb[side, t, h, b, j] for side, b, _ in places], axis=0)

    def query_side(h):
        lane = lax.broadcasted_iota(jnp.int32, (rows, 128), 1)
        table = jnp.zeros((rows, 128), jnp.float32)
        for a in range(ROW):
            places = readers(a, 1)
            keys, values = stacked(KV, h, 0, places), stacked(KV, h, 1, places)
            queries, grads = rb[OWN, QG, h, a, 0], rb[OWN, QG, h, a, 1]
            shift = jnp.concatenate([bias[OWN, a, d:d + 1, :] for _, _, d in places], axis=1)
            scores = lax.dot_general(queries, keys, NT, preferred_element_type=jnp.float32)
            scores = scores * scale - shift
            top = jnp.max(scores, axis=1, keepdims=True)
            weights = jnp.exp(scores - top)
            total = jnp.sum(weights, axis=1, keepdims=True)
            exact = weights * (1.0 / total)
            out = jnp.dot(exact.astype(jnp.bfloat16), values, preferred_element_type=jnp.float32)
            out = out.astype(jnp.bfloat16)
            held[OUT, h, a] = out
            delta = jnp.sum(grads.astype(jnp.float32) * out.astype(jnp.float32), axis=1, keepdims=True)
            dprobs = lax.dot_general(grads, values, NT, preferred_element_type=jnp.float32)
            dscores = (exact * (dprobs - delta)).astype(jnp.bfloat16)
            grad = jnp.dot(dscores, keys, preferred_element_type=jnp.float32) * scale
            held[GQ, h, a] = grad.astype(jnp.bfloat16)
            table = jnp.where(lane == a, top + jnp.log(total), table)
            table = jnp.where(lane == a + ROW, delta, table)
        stats[OWN, h] = jnp.transpose(table)[:2 * ROW]
        for side in (UP, DN):
            @pl.when(exists[side])
            def _(side=side):
                stat_copy(side, other[side], h).start()
        give_back(OUT, h)
        give_back(GQ, h)

    def key_side(h):
        for side in (UP, DN):
            @pl.when(exists[side])
            def _(side=side):
                stat_copy(side, side, h).wait_recv()
        for b in range(ROW):
            places = readers(b, -1)
            queries, grads = stacked(QG, h, 0, places), stacked(QG, h, 1, places)
            keys, values = rb[OWN, KV, h, b, 0], rb[OWN, KV, h, b, 1]
            lse = jnp.concatenate(
                [stats[side, h, a:a + 1] + bias[side, a, d:d + 1] for side, a, d in places], axis=1
            )
            delta = jnp.concatenate([stats[side, h, a + ROW:a + ROW + 1] for side, a, _ in places], axis=1)
            scores = lax.dot_general(keys, queries, NT, preferred_element_type=jnp.float32)
            exact = jnp.exp(scores * scale - lse)
            value_grad = jnp.dot(exact.astype(jnp.bfloat16), grads, preferred_element_type=jnp.float32)
            held[GV, h, b] = value_grad.astype(jnp.bfloat16)
            dprobs = lax.dot_general(values, grads, NT, preferred_element_type=jnp.float32)
            dscores = (exact * (dprobs - delta)).astype(jnp.bfloat16)
            key_grad = jnp.dot(dscores, queries, preferred_element_type=jnp.float32) * scale
            held[GK, h, b] = key_grad.astype(jnp.bfloat16)
        give_back(GK, h)
        give_back(GV, h)

    pl.semaphore_wait(barrier, 3 + sum(jnp.where(exists[side], 1, 0) for side in (UP, DN)))

    exchange(KV, 0)
    forward(0, KV, 0)
    exchange(QG, 0)
    forward(0, QG, 0)
    for m in (1, 2, 3):
        bias_copy(m, place).start()
    forward(1, KV, 0)
    forward(1, QG, 0)
    exchange(KV, 1)
    exchange(QG, 1)

    for side in (UP, DN):
        @pl.when(jnp.logical_not(exists[side]))
        def _(side=side):
            rb[side] = jnp.zeros(rb.shape[1:], rb.dtype)
            stats[side] = jnp.zeros(stats.shape[1:], jnp.float32)
            bias[side] = jnp.full(bias.shape[1:], BIG, jnp.float32)

    for m in (2, 3):
        forward(m, KV, 0)
    for m in (2, 3):
        forward(m, QG, 0)
    for m in (1, 2, 3):
        bias_copy(m, mates[m]).wait_recv()
    for side in (UP, DN):
        @pl.when(exists[side])
        def _(side=side):
            zbias_copy(side, other[side]).start()
    for side in (UP, DN):
        @pl.when(exists[side])
        def _(side=side):
            zbias_copy(side, side).wait_recv()

    def step(h, carry):
        more = h + 1 < heads

        @pl.when(h + 2 < heads)
        def _():
            exchange(KV, h + 2)
            exchange(QG, h + 2)

        @pl.when(more)
        def _():
            for m in range(ROW):
                forward(m, KV, h + 1)

        z_arrived(KV, h)
        query_side(h)

        @pl.when(more)
        def _():
            for m in range(ROW):
                forward(m, QG, h + 1)

        z_arrived(QG, h)
        key_side(h)
        return carry

    lax.fori_loop(0, heads, step, 0)

    for m in (1, 2, 3):
        bias_copy(m, place).wait_send()
    for side in (UP, DN):
        @pl.when(exists[side])
        def _(side=side):
            zbias_copy(side, other[side]).wait_send()

    def drain(h, carry):
        for t in (KV, QG):
            for m in (1, 2, 3):
                row_pair(m, t, h).wait_send()
        for side in (UP, DN):
            @pl.when(exists[side])
            def _(side=side):
                for t in (KV, QG):
                    z_whole(side, t, h).wait_send()
                stat_copy(side, other[side], h).wait_send()
        for j in range(4):
            three = held.at[j, h, pl.ds(0, 3)]
            remote(three, three, ret_send.at[j, h], ret_recv.at[0], first + mates[1]).wait_send()
            own_copy(j, h).wait()
        return carry

    lax.fori_loop(0, heads, drain, 0)

    for m in (1, 2, 3):
        block = out_ref.at[:, :, pl.ds(0, heads * HEAD)]
        remote(block, block, ret_send.at[0, 0], ret_recv.at[m - 1], first + mates[m]).wait_recv()


def local(seq, query, key, value, grad_out, tile_mask):
    rows, features = query.shape
    heads = features // HEAD // ROW
    anywhere = pl.BlockSpec(memory_space=pl.ANY)
    pairs = rows * rows * features * 7
    dma = pltpu.SemaphoreType.DMA
    results = pl.pallas_call(
        functools.partial(kernel, seq),
        name="radial",
        out_shape=jax.ShapeDtypeStruct((4, rows, features), jnp.bfloat16),
        in_specs=[pl.BlockSpec(memory_space=pltpu.SMEM)] + [anywhere] * 4,
        out_specs=pl.BlockSpec(memory_space=pltpu.HBM),
        scratch_shapes=[
            pltpu.VMEM((3, 2, heads, ROW, 2, rows, HEAD), jnp.bfloat16),
            pltpu.VMEM((4, heads, ROW, rows, HEAD), jnp.bfloat16),
            pltpu.VMEM((3, ROW, 8, 128), jnp.float32),
            pltpu.VMEM((3, heads, 8, 128), jnp.float32),
            dma((2, heads)),
            dma((2, heads, 3)), dma((2, heads, 3)),
            dma((3, 2, heads)), dma((3, 2, heads)),
            dma((3,)), dma((3,)), dma((3,)), dma((3,)),
            dma((3, heads)), dma((3, heads)),
            dma((4, heads)), dma((4, heads)), dma((3,)),
        ],
        compiler_params=pltpu.CompilerParams(
            collective_id=0, has_side_effects=True, vmem_limit_bytes=62 << 20
        ),
        cost_estimate=pl.CostEstimate(
            flops=16 * pairs, transcendentals=2 * pairs // HEAD, bytes_accessed=16 * rows * features
        ),
    )(tile_mask.reshape(7), query, key, value, grad_out)
    return tuple(results[j] for j in range(4))


def solution(mesh):
    spec = P(("grp", "seq"), None)
    return jax.shard_map(
        functools.partial(local, mesh.shape["seq"]),
        mesh=mesh,
        in_specs=(spec,) * 4 + (P("seq", None, None, None),),
        out_specs=(spec,) * 4,
        check_vma=False,
    )
```

```python
import functools

import jax
import jax.numpy as jnp
from jax import lax
from jax.experimental import pallas as pl
from jax.experimental.pallas import tpu as pltpu
from jax.sharding import PartitionSpec as P

HEAD = 128
ROW = 4
BIG = 1e30
DIST = {0: 0, 1: 1, -1: 2, 2: 3, -2: 4, 4: 5, -4: 6}

OWN, UP, DN = range(3)
KV, QG = range(2)
OUT, GQ, GK, GV = range(4)
SHIFT = {OWN: 0, UP: ROW, DN: -ROW}
NT = (((1,), (1,)), ((), ()))


def readers(a, sign):
    found = []
    for side in (OWN, UP, DN):
        for b in range(ROW):
            offset = sign * (SHIFT[side] + b - a)
            if offset in DIST:
                found.append((side, b, DIST[offset]))
    return found


ORDER = {UP: (2, 3, 0, 1), DN: (0, 2, 1, 3)}
TURNS = (2, 0, 3, 1)
MIRROR = (0, 2, 1, 4, 3, 6, 5)


def kernel(seq, mask_ref, q_ref, k_ref, v_ref, g_ref, out_ref,
           rb, held, bias, turned, stats,
           load_sem, row_send, row_recv, z_send, z_recv, bias_send, bias_recv, zbias_send, zbias_recv,
           stat_send, stat_recv, own_sem, ret_send, ret_recv):
    rows = q_ref.shape[0]
    heads = q_ref.shape[1] // HEAD // ROW
    scale = HEAD ** (-0.5)
    sources = ((k_ref, v_ref), (q_ref, g_ref))

    me = lax.axis_index("seq")
    place = lax.rem(me, ROW)
    first = me - place
    flip = lax.div(place, 2)

    def real(shard):
        return shard + flip * (3 - 2 * shard)

    mine = real(place)
    beside = 1 - mine
    mates = ((0, beside, mine), (1, 2, 3 - mine), (2, 3, 3 - mine))
    target = {UP: me + ROW * (1 - 2 * flip), DN: me - ROW * (1 - 2 * flip)}
    exists = {side: jnp.logical_and(target[side] >= 0, target[side] < seq) for side in (UP, DN)}
    other = {UP: DN, DN: UP}
    held_by = {OWN: OWN, **{side: jnp.where(exists[side], side, OWN) for side in (UP, DN)}}

    def remote(src, dst, send, recv, device):
        return pltpu.make_async_remote_copy(
            src_ref=src, dst_ref=dst, send_sem=send, recv_sem=recv,
            device_id={"seq": device}, device_id_type=pl.DeviceIdType.MESH,
        )

    def at_sides(action):
        for side in (UP, DN):
            @pl.when(exists[side])
            def _(side=side):
                action(side)

    def columns(part, h):
        return pl.ds(pl.multiple_of((part * heads + h) * HEAD, HEAD), HEAD)

    barrier = pltpu.get_barrier_semaphore()
    for _, shard, _ in mates:
        pl.semaphore_signal(barrier, inc=1, device_id={"seq": first + real(shard)})
    at_sides(lambda side: pl.semaphore_signal(barrier, inc=1, device_id={"seq": target[side]}))

    def load(h, carry):
        for t in (KV, QG):
            for j in range(2):
                pltpu.make_async_copy(
                    sources[t][j].at[:, columns(place, h)], rb.at[OWN, t, h, mine, j], load_sem.at[t, h]
                ).start()
        return carry

    lax.fori_loop(0, heads, load, 0)

    index = lax.broadcasted_iota(jnp.int32, (8, 128), 0)
    straight = jnp.zeros((8, 128), jnp.float32)
    mirrored = straight
    for d in range(7):
        straight = jnp.where(index == d, (1.0 - mask_ref[d].astype(jnp.float32)) * BIG, straight)
        mirrored = jnp.where(index == d, (1.0 - mask_ref[MIRROR[d]].astype(jnp.float32)) * BIG, mirrored)
    bias[OWN, mine] = jnp.where(flip == 0, straight, mirrored)
    turned[...] = jnp.where(flip == 0, mirrored, straight)

    def row_copy(mate, t, h, j):
        kind, shard, there = mate
        return remote(
            sources[t][j].at[:, columns(real(shard), h)], rb.at[OWN, t, h, there, j],
            row_send.at[t, h, kind], row_recv.at[t, h, there], first + real(shard),
        )

    def row_pair(mate, t, h):
        kind, shard, _ = mate
        pair = rb.at[OWN, t, h, shard]
        return remote(pair, pair, row_send.at[t, h, kind], row_recv.at[t, h, shard], first + real(shard))

    def bias_copy(mate):
        kind, shard, there = mate
        src = bias.at[OWN, mine] if kind == 0 else turned
        return remote(src, bias.at[OWN, there], bias_send.at[kind], bias_recv.at[there], first + real(shard))

    def bias_arrival(mate):
        kind, shard, _ = mate
        tile = bias.at[OWN, shard]
        return remote(tile, tile, bias_send.at[kind], bias_recv.at[shard], first + real(shard))

    def zbias_copy(side, landing):
        return remote(bias.at[OWN], bias.at[landing], zbias_send.at[side], zbias_recv.at[landing], target[side])

    def z_copy(side, t, h, shard):
        return remote(
            rb.at[OWN, t, h, shard], rb.at[other[side], t, h, shard],
            z_send.at[side, t, h], z_recv.at[other[side], t, h, shard], target[side],
        )

    def z_arrival(side, t, h, shard):
        return remote(
            rb.at[OWN, t, h, shard], rb.at[side, t, h, shard],
            z_send.at[side, t, h], z_recv.at[side, t, h, shard], target[side],
        )

    def z_whole(side, t, h):
        return remote(
            rb.at[OWN, t, h], rb.at[side, t, h], z_send.at[side, t, h], z_recv.at[side, t, h, 0], target[side]
        )

    def stat_copy(side, landing, h):
        return remote(
            stats.at[OWN, h], stats.at[landing, h], stat_send.at[side, h], stat_recv.at[landing, h], target[side]
        )

    def exchange(mate, t, h):
        for j in range(2):
            row_copy(mate, t, h, j).start()

    def loaded(t, h):
        pair = rb.at[OWN, t, h, mine]
        pltpu.make_async_copy(pair, pair, load_sem.at[t, h]).wait()

    def row_arrived(t, h):
        loaded(t, h)
        for mate in mates:
            row_pair(mate, t, h).wait_recv()

    def z_items(t, h, items):
        def both(side):
            for i in items:
                z_copy(side, t, h, ORDER[side][i]).start()
        at_sides(both)

    def z_shard(t, h, shard):
        at_sides(lambda side: z_copy(side, t, h, shard).start())

    def give_back(j, h, shard):
        block = held.at[j, h, shard]
        cols = out_ref.at[j, :, columns(place, h)]
        if shard >= 2:
            remote(block, cols, ret_send.at[h], ret_recv.at[3 - mine], first + real(shard)).start()
        else:
            @pl.when(mine == shard)
            def _():
                pltpu.make_async_copy(block, cols, own_sem.at[h]).start()

            @pl.when(mine != shard)
            def _():
                remote(block, cols, ret_send.at[h], ret_recv.at[mine], first + real(beside)).start()

    def stacked(t, h, j, places):
        return jnp.concatenate([rb[held_by[side], t, h, b, j] for side, b, _ in places], axis=0)

    def needs(t, h, places, ready):
        for side in (UP, DN):
            new = [b for s, b, _ in places if s == side and (s, b) not in ready]
            ready.update((side, b) for b in new)
            if new:
                @pl.when(exists[side])
                def _(side=side, new=new):
                    for b in new:
                        z_arrival(side, t, h, b).wait_recv()

    def query_side(h):
        lane = lax.broadcasted_iota(jnp.int32, (rows, 128), 1)
        table = jnp.zeros((rows, 128), jnp.float32)
        ready = set()
        for a in TURNS:
            places = readers(a, 1)
            needs(KV, h, places, ready)
            keys, values = stacked(KV, h, 0, places), stacked(KV, h, 1, places)
            queries, grads = rb[OWN, QG, h, a, 0], rb[OWN, QG, h, a, 1]
            shift = jnp.concatenate([bias[OWN, a, d:d + 1, :] for _, _, d in places], axis=1)
            scores = lax.dot_general(queries, keys, NT, preferred_element_type=jnp.float32)
            scores = scores * scale - shift
            top = jnp.max(scores, axis=1, keepdims=True)
            weights = jnp.exp(scores - top)
            total = jnp.sum(weights, axis=1, keepdims=True)
            exact = weights * (1.0 / total)
            out = jnp.dot(exact.astype(jnp.bfloat16), values, preferred_element_type=jnp.float32)
            out = out.astype(jnp.bfloat16)
            held[OUT, h, a] = out
            delta = jnp.sum(grads.astype(jnp.float32) * out.astype(jnp.float32), axis=1, keepdims=True)
            dprobs = lax.dot_general(grads, values, NT, preferred_element_type=jnp.float32)
            dscores = (exact * (dprobs - delta)).astype(jnp.bfloat16)
            grad = jnp.dot(dscores, keys, preferred_element_type=jnp.float32) * scale
            held[GQ, h, a] = grad.astype(jnp.bfloat16)
            table = jnp.where(lane == a, top + jnp.log(total), table)
            table = jnp.where(lane == a + ROW, delta, table)
            give_back(OUT, h, a)
            give_back(GQ, h, a)
        stats[OWN, h] = jnp.transpose(table)[:2 * ROW]
        at_sides(lambda side: stat_copy(side, other[side], h).start())

    def key_side(h):
        at_sides(lambda side: stat_copy(side, side, h).wait_recv())
        ready = set()
        for b in TURNS:
            places = readers(b, -1)
            needs(QG, h, places, ready)
            queries, grads = stacked(QG, h, 0, places), stacked(QG, h, 1, places)
            keys, values = rb[OWN, KV, h, b, 0], rb[OWN, KV, h, b, 1]
            lse = jnp.concatenate(
                [stats[side, h, a:a + 1] + bias[side, a, d:d + 1] for side, a, d in places], axis=1
            )
            delta = jnp.concatenate([stats[side, h, a + ROW:a + ROW + 1] for side, a, _ in places], axis=1)
            scores = lax.dot_general(keys, queries, NT, preferred_element_type=jnp.float32)
            exact = jnp.exp(scores * scale - lse)
            value_grad = jnp.dot(exact.astype(jnp.bfloat16), grads, preferred_element_type=jnp.float32)
            held[GV, h, b] = value_grad.astype(jnp.bfloat16)
            give_back(GV, h, b)
            dprobs = lax.dot_general(values, grads, NT, preferred_element_type=jnp.float32)
            dscores = (exact * (dprobs - delta)).astype(jnp.bfloat16)
            key_grad = jnp.dot(dscores, queries, preferred_element_type=jnp.float32) * scale
            held[GK, h, b] = key_grad.astype(jnp.bfloat16)
            give_back(GK, h, b)

    pl.semaphore_wait(barrier, 3 + sum(jnp.where(exists[side], 1, 0) for side in (UP, DN)))

    for mate in mates:
        bias_copy(mate).start()
    for h in range(2):
        loaded(KV, h)
        z_shard(KV, h, mine)
    for t, h in ((KV, 0), (KV, 1), (QG, 0)):
        for mate in mates:
            exchange(mate, t, h)
    for h in range(2):
        row_pair(mates[0], KV, h).wait_recv()
        z_shard(KV, h, beside)

    def exchange_rest(h, carry):
        @pl.when(h < heads)
        def _():
            for mate in mates:
                exchange(mate, KV, h)
        for mate in mates:
            exchange(mate, QG, h - 1)
        return carry

    lax.fori_loop(2, heads + 1, exchange_rest, 0)

    for side in (UP, DN):
        @pl.when(jnp.logical_not(exists[side]))
        def _(side=side):
            stats[side] = jnp.zeros(stats.shape[1:], jnp.float32)
            bias[side] = jnp.full(bias.shape[1:], BIG, jnp.float32)

    for h in range(2):
        for mate in mates[1:]:
            row_pair(mate, KV, h).wait_recv()
            z_shard(KV, h, mate[1])
    for mate in mates:
        bias_arrival(mate).wait_recv()
    at_sides(lambda side: zbias_copy(side, other[side]).start())
    row_arrived(QG, 0)
    z_items(QG, 0, (0, 1, 2, 3))

    def step(i, carry):
        @pl.when(jnp.logical_and(i >= 1, i + 1 < heads))
        def _():
            row_arrived(KV, i + 1)
            z_items(KV, i + 1, (0, 1, 2, 3))

        @pl.when(jnp.logical_and(i >= 1, i < heads))
        def _():
            row_arrived(QG, i)

        @pl.when(i < heads)
        def _():
            query_side(i)

        @pl.when(jnp.logical_and(i >= 1, i < heads))
        def _():
            z_items(QG, i, (0, 1, 2, 3))

        @pl.when(i == 1)
        def _():
            at_sides(lambda side: zbias_copy(side, side).wait_recv())

        @pl.when(i >= 1)
        def _():
            drain_early(i - 1)
            key_side(i - 1)

        return carry

    def drain_early(h):
        for t in (KV, QG):
            for mate in mates:
                row_pair(mate, t, h).wait_send()

        def sent(side):
            z_whole(side, KV, h).wait_send()
            stat_copy(side, other[side], h).wait_send()

        at_sides(sent)

    lax.fori_loop(0, heads + 1, step, 0)

    for mate in mates:
        bias_copy(mate).wait_send()
    at_sides(lambda side: zbias_copy(side, other[side]).wait_send())

    def drain(h, carry):
        at_sides(lambda side: z_whole(side, QG, h).wait_send())
        blocks = held.at[pl.ds(0, 3), h]
        remote(blocks, blocks, ret_send.at[h], ret_recv.at[0], first + real(2)).wait_send()
        four = held.at[:, h, 0]
        pltpu.make_async_copy(four, four, own_sem.at[h]).wait()
        return carry

    lax.fori_loop(0, heads, drain, 0)

    for _, shard, _ in mates:
        block = out_ref.at[:, :, pl.ds(0, heads * HEAD)]
        remote(block, block, ret_send.at[0], ret_recv.at[shard], first + real(shard)).wait_recv()


def local(seq, query, key, value, grad_out, tile_mask):
    rows, features = query.shape
    heads = features // HEAD // ROW
    anywhere = pl.BlockSpec(memory_space=pl.ANY)
    pairs = rows * rows * features * 7
    dma = pltpu.SemaphoreType.DMA
    results = pl.pallas_call(
        functools.partial(kernel, seq),
        name="radial",
        out_shape=jax.ShapeDtypeStruct((4, rows, features), jnp.bfloat16),
        in_specs=[pl.BlockSpec(memory_space=pltpu.SMEM)] + [anywhere] * 4,
        out_specs=pl.BlockSpec(memory_space=pltpu.HBM),
        scratch_shapes=[
            pltpu.VMEM((3, 2, heads, ROW, 2, rows, HEAD), jnp.bfloat16),
            pltpu.VMEM((4, heads, ROW, rows, HEAD), jnp.bfloat16),
            pltpu.VMEM((3, ROW, 8, 128), jnp.float32),
            pltpu.VMEM((8, 128), jnp.float32),
            pltpu.VMEM((3, heads, 8, 128), jnp.float32),
            dma((2, heads)),
            dma((2, heads, 3)), dma((2, heads, ROW)),
            dma((3, 2, heads)), dma((3, 2, heads, ROW)),
            dma((3,)), dma((ROW,)), dma((3,)), dma((3,)),
            dma((3, heads)), dma((3, heads)),
            dma((heads,)), dma((heads,)), dma((ROW,)),
        ],
        compiler_params=pltpu.CompilerParams(
            collective_id=0, has_side_effects=True, vmem_limit_bytes=62 << 20
        ),
        cost_estimate=pl.CostEstimate(
            flops=16 * pairs, transcendentals=2 * pairs // HEAD, bytes_accessed=16 * rows * features
        ),
    )(tile_mask.reshape(7), query, key, value, grad_out)
    return tuple(results[j] for j in range(4))


def solution(mesh):
    spec = P(("grp", "seq"), None)
    return jax.shard_map(
        functools.partial(local, mesh.shape["seq"]),
        mesh=mesh,
        in_specs=(spec,) * 4 + (P("seq", None, None, None),),
        out_specs=(spec,) * 4,
        check_vma=False,
    )
```

```python
import functools

import jax
import jax.numpy as jnp
from jax import lax
from jax.experimental import pallas as pl
from jax.experimental.pallas import tpu as pltpu
from jax.sharding import PartitionSpec as P

HEAD = 128
ROW = 4
BIG = 1e30
DIST = {0: 0, 1: 1, -1: 2, 2: 3, -2: 4, 4: 5, -4: 6}

OWN, UP, DN = range(3)
KV, QG = range(2)
OUT, GQ, GK, GV = range(4)
SHIFT = {OWN: 0, UP: ROW, DN: -ROW}
NT = (((1,), (1,)), ((), ()))


def readers(a, sign):
    found = []
    for side in (OWN, UP, DN):
        for b in range(ROW):
            offset = sign * (SHIFT[side] + b - a)
            if offset in DIST:
                found.append((side, b, DIST[offset]))
    return found


ORDER = {UP: (2, 3, 0, 1), DN: (0, 2, 1, 3)}
TURNS = (2, 0, 3, 1)
MIRROR = (0, 2, 1, 4, 3, 6, 5)


def kernel(seq, mask_hbm, q_ref, k_ref, v_ref, g_ref, att_ref, gq_ref, gk_ref, gv_ref,
           mask_ref, mask_sem, rb, held, bias, turned, stats,
           load_sem, row_send, row_recv, z_send, z_recv, bias_send, bias_recv, zbias_send, zbias_recv,
           stat_send, stat_recv, own_sem, ret_send, ret_recv):
    rows = q_ref.shape[0]
    heads = q_ref.shape[1] // HEAD // ROW
    scale = HEAD ** (-0.5)
    sources = ((k_ref, v_ref), (q_ref, g_ref))
    results = (att_ref, gq_ref, gk_ref, gv_ref)

    me = lax.axis_index("seq")
    place = lax.rem(me, ROW)
    first = me - place
    flip = lax.div(place, 2)

    def real(shard):
        return shard + flip * (3 - 2 * shard)

    mine = real(place)
    beside = 1 - mine
    mates = ((0, beside, mine), (1, 2, 3 - mine), (2, 3, 3 - mine))
    target = {UP: me + ROW * (1 - 2 * flip), DN: me - ROW * (1 - 2 * flip)}
    exists = {side: jnp.logical_and(target[side] >= 0, target[side] < seq) for side in (UP, DN)}
    other = {UP: DN, DN: UP}
    held_by = {OWN: OWN, **{side: jnp.where(exists[side], side, OWN) for side in (UP, DN)}}

    def remote(src, dst, send, recv, device):
        return pltpu.make_async_remote_copy(
            src_ref=src, dst_ref=dst, send_sem=send, recv_sem=recv,
            device_id={"seq": device}, device_id_type=pl.DeviceIdType.MESH,
        )

    def at_sides(action):
        for side in (UP, DN):
            @pl.when(exists[side])
            def _(side=side):
                action(side)

    def columns(part, h):
        return pl.ds(pl.multiple_of((part * heads + h) * HEAD, HEAD), HEAD)

    pltpu.make_async_copy(mask_hbm, mask_ref, mask_sem).start()
    barrier = pltpu.get_barrier_semaphore()
    for _, shard, _ in mates:
        pl.semaphore_signal(barrier, inc=1, device_id={"seq": first + real(shard)})
    at_sides(lambda side: pl.semaphore_signal(barrier, inc=1, device_id={"seq": target[side]}))

    def load(h, carry):
        for t in (KV, QG):
            for j in range(2):
                pltpu.make_async_copy(
                    sources[t][j].at[:, columns(place, h)], rb.at[OWN, t, h, mine, j], load_sem.at[t, h]
                ).start()
        return carry

    lax.fori_loop(0, heads, load, 0)

    pltpu.make_async_copy(mask_hbm, mask_ref, mask_sem).wait()
    index = lax.broadcasted_iota(jnp.int32, (8, 128), 0)
    straight = jnp.zeros((8, 128), jnp.float32)
    mirrored = straight
    for d in range(7):
        straight = jnp.where(index == d, (1.0 - mask_ref[d].astype(jnp.float32)) * BIG, straight)
        mirrored = jnp.where(index == d, (1.0 - mask_ref[MIRROR[d]].astype(jnp.float32)) * BIG, mirrored)
    bias[OWN, mine] = jnp.where(flip == 0, straight, mirrored)
    turned[...] = jnp.where(flip == 0, mirrored, straight)

    def row_copy(mate, t, h, j):
        kind, shard, there = mate
        return remote(
            sources[t][j].at[:, columns(real(shard), h)], rb.at[OWN, t, h, there, j],
            row_send.at[t, h, kind], row_recv.at[t, h, there], first + real(shard),
        )

    def row_pair(mate, t, h):
        kind, shard, _ = mate
        pair = rb.at[OWN, t, h, shard]
        return remote(pair, pair, row_send.at[t, h, kind], row_recv.at[t, h, shard], first + real(shard))

    def bias_copy(mate):
        kind, shard, there = mate
        src = bias.at[OWN, mine] if kind == 0 else turned
        return remote(src, bias.at[OWN, there], bias_send.at[kind], bias_recv.at[there], first + real(shard))

    def bias_arrival(mate):
        kind, shard, _ = mate
        tile = bias.at[OWN, shard]
        return remote(tile, tile, bias_send.at[kind], bias_recv.at[shard], first + real(shard))

    def zbias_copy(side, landing):
        return remote(bias.at[OWN], bias.at[landing], zbias_send.at[side], zbias_recv.at[landing], target[side])

    def z_copy(side, t, h, shard):
        return remote(
            rb.at[OWN, t, h, shard], rb.at[other[side], t, h, shard],
            z_send.at[side, t, h], z_recv.at[other[side], t, h, shard], target[side],
        )

    def z_arrival(side, t, h, shard):
        return remote(
            rb.at[OWN, t, h, shard], rb.at[side, t, h, shard],
            z_send.at[side, t, h], z_recv.at[side, t, h, shard], target[side],
        )

    def z_whole(side, t, h):
        return remote(
            rb.at[OWN, t, h], rb.at[side, t, h], z_send.at[side, t, h], z_recv.at[side, t, h, 0], target[side]
        )

    def stat_copy(side, landing, h):
        return remote(
            stats.at[OWN, h], stats.at[landing, h], stat_send.at[side, h], stat_recv.at[landing, h], target[side]
        )

    def exchange(mate, t, h):
        for j in range(2):
            row_copy(mate, t, h, j).start()

    def loaded(t, h):
        pair = rb.at[OWN, t, h, mine]
        pltpu.make_async_copy(pair, pair, load_sem.at[t, h]).wait()

    def row_arrived(t, h):
        loaded(t, h)
        for mate in mates:
            row_pair(mate, t, h).wait_recv()

    def z_items(t, h, items):
        def both(side):
            for i in items:
                z_copy(side, t, h, ORDER[side][i]).start()
        at_sides(both)

    def z_shard(t, h, shard):
        at_sides(lambda side: z_copy(side, t, h, shard).start())

    def give_back(j, h, shard):
        block = held.at[j, h, shard]
        cols = results[j].at[:, columns(place, h)]
        if shard >= 2:
            remote(block, cols, ret_send.at[h], ret_recv.at[3 - mine], first + real(shard)).start()
        else:
            @pl.when(mine == shard)
            def _():
                pltpu.make_async_copy(block, cols, own_sem.at[h]).start()

            @pl.when(mine != shard)
            def _():
                remote(block, cols, ret_send.at[h], ret_recv.at[mine], first + real(beside)).start()

    def stacked(t, h, j, places):
        return jnp.concatenate([rb[held_by[side], t, h, b, j] for side, b, _ in places], axis=0)

    def needs(t, h, places, ready):
        for side in (UP, DN):
            new = [b for s, b, _ in places if s == side and (s, b) not in ready]
            ready.update((side, b) for b in new)
            if new:
                @pl.when(exists[side])
                def _(side=side, new=new):
                    for b in new:
                        z_arrival(side, t, h, b).wait_recv()

    def query_side(h):
        lane = lax.broadcasted_iota(jnp.int32, (rows, 128), 1)
        table = jnp.zeros((rows, 128), jnp.float32)
        ready = set()
        for a in TURNS:
            places = readers(a, 1)
            needs(KV, h, places, ready)
            keys, values = stacked(KV, h, 0, places), stacked(KV, h, 1, places)
            queries, grads = rb[OWN, QG, h, a, 0], rb[OWN, QG, h, a, 1]
            shift = jnp.concatenate([bias[OWN, a, d:d + 1, :] for _, _, d in places], axis=1)
            scores = lax.dot_general(queries, keys, NT, preferred_element_type=jnp.float32)
            scores = scores * scale - shift
            top = jnp.max(scores, axis=1, keepdims=True)
            weights = jnp.exp(scores - top)
            total = jnp.sum(weights, axis=1, keepdims=True)
            exact = weights * (1.0 / total)
            out = jnp.dot(exact.astype(jnp.bfloat16), values, preferred_element_type=jnp.float32)
            out = out.astype(jnp.bfloat16)
            held[OUT, h, a] = out
            delta = jnp.sum(grads.astype(jnp.float32) * out.astype(jnp.float32), axis=1, keepdims=True)
            dprobs = lax.dot_general(grads, values, NT, preferred_element_type=jnp.float32)
            dscores = (exact * (dprobs - delta)).astype(jnp.bfloat16)
            grad = jnp.dot(dscores, keys, preferred_element_type=jnp.float32) * scale
            held[GQ, h, a] = grad.astype(jnp.bfloat16)
            table = jnp.where(lane == a, top + jnp.log(total), table)
            table = jnp.where(lane == a + ROW, delta, table)
            give_back(OUT, h, a)
            give_back(GQ, h, a)
        stats[OWN, h] = jnp.transpose(table)[:2 * ROW]
        at_sides(lambda side: stat_copy(side, other[side], h).start())

    def key_side(h):
        at_sides(lambda side: stat_copy(side, side, h).wait_recv())
        ready = set()
        for b in TURNS:
            places = readers(b, -1)
            needs(QG, h, places, ready)
            queries, grads = stacked(QG, h, 0, places), stacked(QG, h, 1, places)
            keys, values = rb[OWN, KV, h, b, 0], rb[OWN, KV, h, b, 1]
            lse = jnp.concatenate(
                [stats[side, h, a:a + 1] + bias[side, a, d:d + 1] for side, a, d in places], axis=1
            )
            delta = jnp.concatenate([stats[side, h, a + ROW:a + ROW + 1] for side, a, _ in places], axis=1)
            scores = lax.dot_general(keys, queries, NT, preferred_element_type=jnp.float32)
            exact = jnp.exp(scores * scale - lse)
            value_grad = jnp.dot(exact.astype(jnp.bfloat16), grads, preferred_element_type=jnp.float32)
            held[GV, h, b] = value_grad.astype(jnp.bfloat16)
            give_back(GV, h, b)
            dprobs = lax.dot_general(values, grads, NT, preferred_element_type=jnp.float32)
            dscores = (exact * (dprobs - delta)).astype(jnp.bfloat16)
            key_grad = jnp.dot(dscores, queries, preferred_element_type=jnp.float32) * scale
            held[GK, h, b] = key_grad.astype(jnp.bfloat16)
            give_back(GK, h, b)

    pl.semaphore_wait(barrier, 3 + sum(jnp.where(exists[side], 1, 0) for side in (UP, DN)))

    for mate in mates:
        bias_copy(mate).start()
    for h in range(2):
        loaded(KV, h)
        z_shard(KV, h, mine)
    for t, h in ((KV, 0), (KV, 1), (QG, 0)):
        for mate in mates:
            exchange(mate, t, h)
    for h in range(2):
        row_pair(mates[0], KV, h).wait_recv()
        z_shard(KV, h, beside)

    def exchange_rest(h, carry):
        @pl.when(h < heads)
        def _():
            for mate in mates:
                exchange(mate, KV, h)
        for mate in mates:
            exchange(mate, QG, h - 1)
        return carry

    lax.fori_loop(2, heads + 1, exchange_rest, 0)

    for side in (UP, DN):
        @pl.when(jnp.logical_not(exists[side]))
        def _(side=side):
            stats[side] = jnp.zeros(stats.shape[1:], jnp.float32)
            bias[side] = jnp.full(bias.shape[1:], BIG, jnp.float32)

    for h in range(2):
        for mate in mates[1:]:
            row_pair(mate, KV, h).wait_recv()
            z_shard(KV, h, mate[1])
    for mate in mates:
        bias_arrival(mate).wait_recv()
    at_sides(lambda side: zbias_copy(side, other[side]).start())
    row_arrived(QG, 0)
    z_items(QG, 0, (0, 1, 2, 3))

    def step(i, carry):
        @pl.when(jnp.logical_and(i >= 1, i + 1 < heads))
        def _():
            row_arrived(KV, i + 1)
            z_items(KV, i + 1, (0, 1, 2, 3))

        @pl.when(jnp.logical_and(i >= 1, i < heads))
        def _():
            row_arrived(QG, i)

        @pl.when(i < heads)
        def _():
            query_side(i)

        @pl.when(jnp.logical_and(i >= 1, i < heads))
        def _():
            z_items(QG, i, (0, 1, 2, 3))

        @pl.when(i == 1)
        def _():
            at_sides(lambda side: zbias_copy(side, side).wait_recv())

        @pl.when(i >= 1)
        def _():
            drain_early(i - 1)
            key_side(i - 1)

        return carry

    def drain_early(h):
        for t in (KV, QG):
            for mate in mates:
                row_pair(mate, t, h).wait_send()

        def sent(side):
            z_whole(side, KV, h).wait_send()
            stat_copy(side, other[side], h).wait_send()

        at_sides(sent)

    lax.fori_loop(0, heads + 1, step, 0)

    for mate in mates:
        bias_copy(mate).wait_send()
    at_sides(lambda side: zbias_copy(side, other[side]).wait_send())

    def drain(h, carry):
        at_sides(lambda side: z_whole(side, QG, h).wait_send())
        blocks = held.at[pl.ds(0, 3), h]
        remote(blocks, blocks, ret_send.at[h], ret_recv.at[0], first + real(2)).wait_send()
        four = held.at[:, h, 0]
        pltpu.make_async_copy(four, four, own_sem.at[h]).wait()
        return carry

    lax.fori_loop(0, heads, drain, 0)

    for _, shard, _ in mates:
        block = held.at[0]
        remote(block, block, ret_send.at[0], ret_recv.at[shard], first + real(shard)).wait_recv()


def copy_out(*refs):
    sems = refs[8]
    band = refs[0].shape[0] // 4
    copies = [
        pltpu.make_async_copy(
            refs[j].at[pl.ds(i * band, band)], refs[4 + j].at[pl.ds(i * band, band)], sems.at[j, i]
        )
        for j in range(4) for i in range(4)
    ]
    for copy in copies:
        copy.start()
    for copy in copies:
        copy.wait()


def finish(*arrays):
    return pl.pallas_call(
        copy_out,
        name="finish",
        out_shape=tuple(jax.ShapeDtypeStruct(a.shape, a.dtype) for a in arrays),
        in_specs=[pl.BlockSpec(memory_space=pl.ANY)] * 4,
        out_specs=(pl.BlockSpec(memory_space=pltpu.HBM),) * 4,
        scratch_shapes=[pltpu.SemaphoreType.DMA((4, 4))],
        compiler_params=pltpu.CompilerParams(vmem_limit_bytes=1 << 20),
    )(*arrays)


def local(seq, query, key, value, grad_out, tile_mask):
    rows, features = query.shape
    heads = features // HEAD // ROW
    pairs = rows * rows * features * 7
    dma = pltpu.SemaphoreType.DMA
    results = pl.pallas_call(
        functools.partial(kernel, seq),
        name="radial",
        out_shape=(jax.ShapeDtypeStruct((rows, features), jnp.bfloat16),) * 4,
        in_specs=[pl.BlockSpec(memory_space=pltpu.HBM)] + [pl.BlockSpec(memory_space=pltpu.HBM)] * 4,
        out_specs=(pl.BlockSpec(memory_space=pl.ANY),) * 4,
        scratch_shapes=[
            pltpu.SMEM((7,), jnp.int32),
            dma(()),
            pltpu.VMEM((3, 2, heads, ROW, 2, rows, HEAD), jnp.bfloat16),
            pltpu.VMEM((4, heads, ROW, rows, HEAD), jnp.bfloat16),
            pltpu.VMEM((3, ROW, 8, 128), jnp.float32),
            pltpu.VMEM((8, 128), jnp.float32),
            pltpu.VMEM((3, heads, 8, 128), jnp.float32),
            dma((2, heads)),
            dma((2, heads, 3)), dma((2, heads, ROW)),
            dma((3, 2, heads)), dma((3, 2, heads, ROW)),
            dma((3,)), dma((ROW,)), dma((3,)), dma((3,)),
            dma((3, heads)), dma((3, heads)),
            dma((heads,)), dma((heads,)), dma((ROW,)),
        ],
        compiler_params=pltpu.CompilerParams(
            collective_id=0, has_side_effects=True, vmem_limit_bytes=32 << 20
        ),
        cost_estimate=pl.CostEstimate(
            flops=16 * pairs, transcendentals=2 * pairs // HEAD, bytes_accessed=16 * rows * features
        ),
    )(*(pltpu.with_memory_space_constraint(a, pltpu.HBM) for a in (tile_mask.reshape(7), query, key, value, grad_out)))
    return tuple(finish(*results))


def solution(mesh):
    spec = P(("grp", "seq"), None)
    return jax.shard_map(
        functools.partial(local, mesh.shape["seq"]),
        mesh=mesh,
        in_specs=(spec,) * 4 + (P("seq", None, None, None),),
        out_specs=(spec,) * 4,
        check_vma=False,
    )
```

```python
import functools

import jax
import jax.numpy as jnp
from jax import lax
from jax.experimental import pallas as pl
from jax.experimental.pallas import tpu as pltpu
from jax.sharding import PartitionSpec as P

HEAD = 128
ROW = 4
BIG = 1e30
DIST = {0: 0, 1: 1, -1: 2, 2: 3, -2: 4, 4: 5, -4: 6}

OWN, UP, DN = range(3)
KV, QG = range(2)
OUT, GQ, GK, GV = range(4)
SHIFT = {OWN: 0, UP: ROW, DN: -ROW}
NT = (((1,), (1,)), ((), ()))


def readers(a, sign):
    found = []
    for side in (OWN, UP, DN):
        for b in range(ROW):
            offset = sign * (SHIFT[side] + b - a)
            if offset in DIST:
                found.append((side, b, DIST[offset]))
    return found


ORDER = {UP: (2, 3, 0, 1), DN: (0, 1, 3, 2)}
TURNS = (0, 3, 2, 1)
WHOLE, START, REST = range(3)
LAST = (UP, 2)
KEY_PLAN = ((2, START), (3, WHOLE), (0, WHOLE), (2, REST), (1, WHOLE))
MIRROR = (0, 2, 1, 4, 3, 6, 5)


def kernel(seq, mask_hbm, q_ref, k_ref, v_ref, g_ref, att_ref, gq_ref, gk_ref, gv_ref,
           mask_ref, mask_sem, rb, held, bias, turned, packed, stats,
           load_sem, row_send, row_recv, z_send, z_recv, bias_send, bias_recv, zbias_send, zbias_recv,
           stat_send, stat_recv, own_sem, ret_send, ret_recv):
    rows = q_ref.shape[0]
    heads = q_ref.shape[1] // HEAD // ROW
    scale = HEAD ** (-0.5)
    sources = ((k_ref, v_ref), (q_ref, g_ref))
    results = (att_ref, gq_ref, gk_ref, gv_ref)

    me = lax.axis_index("seq")
    place = lax.rem(me, ROW)
    first = me - place
    flip = lax.div(place, 2)

    def real(shard):
        return shard + flip * (3 - 2 * shard)

    mine = real(place)
    beside = 1 - mine
    mates = ((0, beside, mine), (1, 2, 3 - mine), (2, 3, 3 - mine))
    target = {UP: me + ROW * (1 - 2 * flip), DN: me - ROW * (1 - 2 * flip)}
    exists = {side: jnp.logical_and(target[side] >= 0, target[side] < seq) for side in (UP, DN)}
    other = {UP: DN, DN: UP}
    held_by = {OWN: OWN, **{side: jnp.where(exists[side], side, OWN) for side in (UP, DN)}}

    def remote(src, dst, send, recv, device):
        return pltpu.make_async_remote_copy(
            src_ref=src, dst_ref=dst, send_sem=send, recv_sem=recv,
            device_id={"seq": device}, device_id_type=pl.DeviceIdType.MESH,
        )

    def at_sides(action):
        for side in (UP, DN):
            @pl.when(exists[side])
            def _(side=side):
                action(side)

    def columns(part, h):
        return pl.ds(pl.multiple_of((part * heads + h) * HEAD, HEAD), HEAD)

    pltpu.make_async_copy(mask_hbm, mask_ref, mask_sem).start()
    barrier = pltpu.get_barrier_semaphore()
    for _, shard, _ in mates:
        pl.semaphore_signal(barrier, inc=1, device_id={"seq": first + real(shard)})
    at_sides(lambda side: pl.semaphore_signal(barrier, inc=1, device_id={"seq": target[side]}))

    def load(h, carry):
        for t in (KV, QG):
            for j in range(2):
                pltpu.make_async_copy(
                    sources[t][j].at[:, columns(place, h)], rb.at[OWN, t, h, mine, j], load_sem.at[t, h]
                ).start()
        return carry

    lax.fori_loop(0, heads, load, 0)

    pltpu.make_async_copy(mask_hbm, mask_ref, mask_sem).wait()
    index = lax.broadcasted_iota(jnp.int32, (8, 128), 0)
    straight = jnp.zeros((8, 128), jnp.float32)
    mirrored = straight
    for d in range(7):
        straight = jnp.where(index == d, (1.0 - mask_ref[d].astype(jnp.float32)) * BIG, straight)
        mirrored = jnp.where(index == d, (1.0 - mask_ref[MIRROR[d]].astype(jnp.float32)) * BIG, mirrored)
    bias[OWN, mine] = jnp.where(flip == 0, straight, mirrored)
    turned[...] = jnp.where(flip == 0, mirrored, straight)

    def row_copy(mate, t, h, j):
        kind, shard, there = mate
        return remote(
            sources[t][j].at[:, columns(real(shard), h)], rb.at[OWN, t, h, there, j],
            row_send.at[t, h, kind], row_recv.at[t, h, there], first + real(shard),
        )

    def row_pair(mate, t, h):
        kind, shard, _ = mate
        pair = rb.at[OWN, t, h, shard]
        return remote(pair, pair, row_send.at[t, h, kind], row_recv.at[t, h, shard], first + real(shard))

    def bias_copy(mate):
        kind, shard, there = mate
        src = bias.at[OWN, mine] if kind == 0 else turned
        return remote(src, bias.at[OWN, there], bias_send.at[kind], bias_recv.at[there], first + real(shard))

    def bias_arrival(mate):
        kind, shard, _ = mate
        tile = bias.at[OWN, shard]
        return remote(tile, tile, bias_send.at[kind], bias_recv.at[shard], first + real(shard))

    def zbias_copy(side, landing):
        return remote(packed.at[OWN], packed.at[landing], zbias_send.at[side], zbias_recv.at[landing], target[side])

    def z_copy(side, t, h, shard):
        return remote(
            rb.at[OWN, t, h, shard], rb.at[other[side], t, h, shard],
            z_send.at[side, t, h], z_recv.at[other[side], t, h, shard], target[side],
        )

    def z_arrival(side, t, h, shard):
        return remote(
            rb.at[OWN, t, h, shard], rb.at[side, t, h, shard],
            z_send.at[side, t, h], z_recv.at[side, t, h, shard], target[side],
        )

    def z_whole(side, t, h):
        return remote(
            rb.at[OWN, t, h], rb.at[side, t, h], z_send.at[side, t, h], z_recv.at[side, t, h, 0], target[side]
        )

    def stat_copy(side, landing, h):
        return remote(
            stats.at[OWN, h], stats.at[landing, h], stat_send.at[side, h], stat_recv.at[landing, h], target[side]
        )

    def exchange(mate, t, h):
        for j in range(2):
            row_copy(mate, t, h, j).start()

    def loaded(t, h):
        pair = rb.at[OWN, t, h, mine]
        pltpu.make_async_copy(pair, pair, load_sem.at[t, h]).wait()

    def row_arrived(t, h):
        loaded(t, h)
        for mate in mates:
            row_pair(mate, t, h).wait_recv()

    def z_items(t, h, items):
        def both(side):
            for i in items:
                z_copy(side, t, h, ORDER[side][i]).start()
        at_sides(both)

    def z_shard(t, h, shard):
        at_sides(lambda side: z_copy(side, t, h, shard).start())

    def give_back(j, h, shard):
        block = held.at[j, h, shard]
        cols = results[j].at[:, columns(place, h)]
        if shard >= 2:
            remote(block, cols, ret_send.at[h], ret_recv.at[3 - mine], first + real(shard)).start()
        else:
            @pl.when(mine == shard)
            def _():
                pltpu.make_async_copy(block, cols, own_sem.at[h]).start()

            @pl.when(mine != shard)
            def _():
                remote(block, cols, ret_send.at[h], ret_recv.at[mine], first + real(beside)).start()

    def stacked(t, h, j, places):
        return jnp.concatenate([rb[held_by[side], t, h, b, j] for side, b, _ in places], axis=0)

    def needs(t, h, places, ready):
        for side in (UP, DN):
            new = [b for s, b, _ in places if s == side and (s, b) not in ready]
            ready.update((side, b) for b in new)
            if new:
                @pl.when(exists[side])
                def _(side=side, new=new):
                    for b in new:
                        z_arrival(side, t, h, b).wait_recv()

    def query_side(h):
        lane = lax.broadcasted_iota(jnp.int32, (rows, 128), 1)
        table = jnp.zeros((rows, 128), jnp.float32)
        ready = set()
        for a in TURNS:
            places = readers(a, 1)
            needs(KV, h, places, ready)
            keys, values = stacked(KV, h, 0, places), stacked(KV, h, 1, places)
            queries, grads = rb[OWN, QG, h, a, 0], rb[OWN, QG, h, a, 1]
            shift = jnp.concatenate([bias[OWN, a, d:d + 1, :] for _, _, d in places], axis=1)
            scores = lax.dot_general(queries, keys, NT, preferred_element_type=jnp.float32)
            scores = scores * scale - shift
            top = jnp.max(scores, axis=1, keepdims=True)
            weights = jnp.exp(scores - top)
            total = jnp.sum(weights, axis=1, keepdims=True)
            exact = weights * (1.0 / total)
            out = jnp.dot(exact.astype(jnp.bfloat16), values, preferred_element_type=jnp.float32)
            out = out.astype(jnp.bfloat16)
            held[OUT, h, a] = out
            delta = jnp.sum(grads.astype(jnp.float32) * out.astype(jnp.float32), axis=1, keepdims=True)
            dprobs = lax.dot_general(grads, values, NT, preferred_element_type=jnp.float32)
            dscores = (exact * (dprobs - delta)).astype(jnp.bfloat16)
            grad = jnp.dot(dscores, keys, preferred_element_type=jnp.float32) * scale
            held[GQ, h, a] = grad.astype(jnp.bfloat16)
            table = jnp.where(lane == a, top + jnp.log(total), table)
            table = jnp.where(lane == a + ROW, delta, table)
            give_back(OUT, h, a)
            give_back(GQ, h, a)
        stats[OWN, h] = jnp.transpose(table)[:2 * ROW]
        at_sides(lambda side: stat_copy(side, other[side], h).start())

    def key_terms(h, b, places):
        queries, grads = stacked(QG, h, 0, places), stacked(QG, h, 1, places)
        keys, values = rb[OWN, KV, h, b, 0], rb[OWN, KV, h, b, 1]
        lse = jnp.concatenate(
            [stats[side, h, a:a + 1] + bias[side, a, d:d + 1] for side, a, d in places], axis=1
        )
        delta = jnp.concatenate([stats[side, h, a + ROW:a + ROW + 1] for side, a, _ in places], axis=1)
        scores = lax.dot_general(keys, queries, NT, preferred_element_type=jnp.float32)
        exact = jnp.exp(scores * scale - lse)
        value_grad = jnp.dot(exact.astype(jnp.bfloat16), grads, preferred_element_type=jnp.float32)
        dprobs = lax.dot_general(values, grads, NT, preferred_element_type=jnp.float32)
        dscores = (exact * (dprobs - delta)).astype(jnp.bfloat16)
        return value_grad, jnp.dot(dscores, queries, preferred_element_type=jnp.float32)

    def key_side(h):
        at_sides(lambda side: stat_copy(side, side, h).wait_recv())
        ready = set()
        partial = None
        for b, part in KEY_PLAN:
            places = [place for place in readers(b, -1) if part == WHOLE or (place[:2] == LAST) == (part == REST)]
            needs(QG, h, places, ready)
            terms = key_terms(h, b, places)
            if part == START:
                partial = terms
                continue
            if part == REST:
                terms = [before + more for before, more in zip(partial, terms)]
            held[GV, h, b] = terms[0].astype(jnp.bfloat16)
            give_back(GV, h, b)
            held[GK, h, b] = (terms[1] * scale).astype(jnp.bfloat16)
            give_back(GK, h, b)

    pl.semaphore_wait(barrier, 3 + sum(jnp.where(exists[side], 1, 0) for side in (UP, DN)))

    for mate in mates:
        bias_copy(mate).start()
    for h in range(2):
        loaded(KV, h)

    @pl.when(mine == 0)
    def _():
        for h in range(2):
            z_shard(KV, h, mine)

    for t, h in ((KV, 0), (KV, 1), (QG, 0)):
        for mate in mates:
            exchange(mate, t, h)

    @pl.when(mine == 1)
    def _():
        for h in range(2):
            z_shard(KV, h, mine)

    for h in range(2):
        row_pair(mates[0], KV, h).wait_recv()
        z_shard(KV, h, beside)

    def exchange_rest(h, carry):
        @pl.when(h < heads)
        def _():
            for mate in mates:
                exchange(mate, KV, h)
        for mate in mates:
            exchange(mate, QG, h - 1)
        return carry

    lax.fori_loop(2, heads + 1, exchange_rest, 0)

    for side in (UP, DN):
        @pl.when(jnp.logical_not(exists[side]))
        def _(side=side):
            stats[side] = jnp.zeros(stats.shape[1:], jnp.float32)
            bias[side] = jnp.full(bias.shape[1:], BIG, jnp.float32)

    for h in range(2):
        for mate in mates[1:]:
            row_pair(mate, KV, h).wait_recv()
            z_shard(KV, h, mate[1])
    for mate in mates:
        bias_arrival(mate).wait_recv()
    column = lax.broadcasted_iota(jnp.int32, (8, 128), 1)
    packed[OWN] = functools.reduce(lambda tile, a: jnp.where(column == a, bias[OWN, a], tile), range(1, ROW), bias[OWN, 0])
    at_sides(lambda side: zbias_copy(side, other[side]).start())
    row_arrived(QG, 0)
    z_items(QG, 0, (0, 1, 2, 3))

    def step(i, carry):
        @pl.when(jnp.logical_and(i >= 1, i + 1 < heads))
        def _():
            row_arrived(KV, i + 1)
            z_items(KV, i + 1, (0, 1, 2, 3))

        @pl.when(jnp.logical_and(i >= 1, i < heads))
        def _():
            row_arrived(QG, i)

        @pl.when(i < heads)
        def _():
            query_side(i)

        @pl.when(jnp.logical_and(i >= 1, i < heads))
        def _():
            z_items(QG, i, (0, 1, 2, 3))

        @pl.when(i == 1)
        def _():
            at_sides(unpack)

        @pl.when(i >= 1)
        def _():
            drain_early(i - 1)
            key_side(i - 1)

        return carry

    def unpack(side):
        zbias_copy(side, side).wait_recv()
        for a in range(ROW):
            bias[side, a] = jnp.broadcast_to(packed[side][:, a:a + 1], (8, 128))

    def drain_early(h):
        for t in (KV, QG):
            for mate in mates:
                row_pair(mate, t, h).wait_send()

        def sent(side):
            z_whole(side, KV, h).wait_send()
            stat_copy(side, other[side], h).wait_send()

        at_sides(sent)

    lax.fori_loop(0, heads + 1, step, 0)

    for mate in mates:
        bias_copy(mate).wait_send()
    at_sides(lambda side: zbias_copy(side, other[side]).wait_send())

    def drain(h, carry):
        at_sides(lambda side: z_whole(side, QG, h).wait_send())
        blocks = held.at[pl.ds(0, 3), h]
        remote(blocks, blocks, ret_send.at[h], ret_recv.at[0], first + real(2)).wait_send()
        four = held.at[:, h, 0]
        pltpu.make_async_copy(four, four, own_sem.at[h]).wait()
        return carry

    lax.fori_loop(0, heads, drain, 0)

    for _, shard, _ in mates:
        block = held.at[0]
        remote(block, block, ret_send.at[0], ret_recv.at[shard], first + real(shard)).wait_recv()


def copy_out(*refs):
    sems = refs[8]
    copies = [pltpu.make_async_copy(refs[j], refs[4 + j], sems.at[j]) for j in range(4)]
    for copy in copies:
        copy.start()
    for copy in copies:
        copy.wait()


def finish(*arrays):
    return pl.pallas_call(
        copy_out,
        name="finish",
        out_shape=tuple(jax.ShapeDtypeStruct(a.shape, a.dtype) for a in arrays),
        in_specs=[pl.BlockSpec(memory_space=pl.ANY)] * 4,
        out_specs=(pl.BlockSpec(memory_space=pltpu.HBM),) * 4,
        scratch_shapes=[pltpu.SemaphoreType.DMA((4,))],
        compiler_params=pltpu.CompilerParams(vmem_limit_bytes=1 << 20),
    )(*arrays)


def local(seq, query, key, value, grad_out, tile_mask):
    rows, features = query.shape
    heads = features // HEAD // ROW
    pairs = rows * rows * features * 7
    dma = pltpu.SemaphoreType.DMA
    results = pl.pallas_call(
        functools.partial(kernel, seq),
        name="radial",
        out_shape=(jax.ShapeDtypeStruct((rows, features), jnp.bfloat16),) * 4,
        in_specs=[pl.BlockSpec(memory_space=pltpu.HBM)] + [pl.BlockSpec(memory_space=pltpu.HBM)] * 4,
        out_specs=(pl.BlockSpec(memory_space=pl.ANY),) * 4,
        scratch_shapes=[
            pltpu.SMEM((7,), jnp.int32),
            dma(()),
            pltpu.VMEM((3, 2, heads, ROW, 2, rows, HEAD), jnp.bfloat16),
            pltpu.VMEM((4, heads, ROW, rows, HEAD), jnp.bfloat16),
            pltpu.VMEM((3, ROW, 8, 128), jnp.float32),
            pltpu.VMEM((8, 128), jnp.float32),
            pltpu.VMEM((3, 8, 128), jnp.float32),
            pltpu.VMEM((3, heads, 8, 128), jnp.float32),
            dma((2, heads)),
            dma((2, heads, 3)), dma((2, heads, ROW)),
            dma((3, 2, heads)), dma((3, 2, heads, ROW)),
            dma((3,)), dma((ROW,)), dma((3,)), dma((3,)),
            dma((3, heads)), dma((3, heads)),
            dma((heads,)), dma((heads,)), dma((ROW,)),
        ],
        compiler_params=pltpu.CompilerParams(
            collective_id=0, has_side_effects=True, vmem_limit_bytes=32 << 20
        ),
        cost_estimate=pl.CostEstimate(
            flops=16 * pairs, transcendentals=2 * pairs // HEAD, bytes_accessed=16 * rows * features
        ),
    )(*(pltpu.with_memory_space_constraint(a, pltpu.HBM) for a in (tile_mask.reshape(7), query, key, value, grad_out)))
    return tuple(finish(*results))


def solution(mesh):
    spec = P(("grp", "seq"), None)
    return jax.shard_map(
        functools.partial(local, mesh.shape["seq"]),
        mesh=mesh,
        in_specs=(spec,) * 4 + (P("seq", None, None, None),),
        out_specs=(spec,) * 4,
        check_vma=False,
    )
```

```python
import functools

import jax
import jax.numpy as jnp
from jax import lax
from jax.experimental import pallas as pl
from jax.experimental.pallas import tpu as pltpu
from jax.sharding import PartitionSpec as P

HEAD = 128
ROW = 4
BIG = 1e30
DIST = {0: 0, 1: 1, -1: 2, 2: 3, -2: 4, 4: 5, -4: 6}

OWN, UP, DN = range(3)
KV, QG = range(2)
OUT, GQ, GK, GV = range(4)
SHIFT = {OWN: 0, UP: ROW, DN: -ROW}
NT = (((1,), (1,)), ((), ()))


def readers(a, sign):
    found = []
    for side in (OWN, UP, DN):
        for b in range(ROW):
            offset = sign * (SHIFT[side] + b - a)
            if offset in DIST:
                found.append((side, b, DIST[offset]))
    return found


ORDER = {UP: (2, 3, 0, 1), DN: (0, 1, 3, 2)}
TURNS = (0, 3, 2, 1)
WHOLE, START, REST = range(3)
LAST = {2: (UP, 2), 3: (UP, 3)}
KEY_PLAN = ((2, START), (3, START), (3, REST), (0, WHOLE), (2, REST), (1, WHOLE))
MIRROR = (0, 2, 1, 4, 3, 6, 5)


def kernel(seq, mask_hbm, q_ref, k_ref, v_ref, g_ref, att_ref, gq_ref, gk_ref, gv_ref,
           mask_ref, mask_sem, rb, held, bias, turned, packed, stats,
           load_sem, row_send, row_recv, z_send, z_recv, bias_send, bias_recv, zbias_send, zbias_recv,
           stat_send, stat_recv, own_sem, ret_send, ret_recv):
    rows = q_ref.shape[0]
    heads = q_ref.shape[1] // HEAD // ROW
    scale = HEAD ** (-0.5)
    sources = ((k_ref, v_ref), (q_ref, g_ref))
    results = (att_ref, gq_ref, gk_ref, gv_ref)

    me = lax.axis_index("seq")
    place = lax.rem(me, ROW)
    first = me - place
    flip = lax.div(place, 2)

    def real(shard):
        return shard + flip * (3 - 2 * shard)

    mine = real(place)
    beside = 1 - mine
    mates = ((0, beside, mine), (1, 2, 3 - mine), (2, 3, 3 - mine))
    target = {UP: me + ROW * (1 - 2 * flip), DN: me - ROW * (1 - 2 * flip)}
    exists = {side: jnp.logical_and(target[side] >= 0, target[side] < seq) for side in (UP, DN)}
    other = {UP: DN, DN: UP}
    held_by = {OWN: OWN, **{side: jnp.where(exists[side], side, OWN) for side in (UP, DN)}}

    def remote(src, dst, send, recv, device):
        return pltpu.make_async_remote_copy(
            src_ref=src, dst_ref=dst, send_sem=send, recv_sem=recv,
            device_id={"seq": device}, device_id_type=pl.DeviceIdType.MESH,
        )

    def at_sides(action):
        for side in (UP, DN):
            @pl.when(exists[side])
            def _(side=side):
                action(side)

    def columns(part, h):
        return pl.ds(pl.multiple_of((part * heads + h) * HEAD, HEAD), HEAD)

    pltpu.make_async_copy(mask_hbm, mask_ref, mask_sem).start()
    barrier = pltpu.get_barrier_semaphore()
    for _, shard, _ in mates:
        pl.semaphore_signal(barrier, inc=1, device_id={"seq": first + real(shard)})
    at_sides(lambda side: pl.semaphore_signal(barrier, inc=1, device_id={"seq": target[side]}))

    def load(h, carry):
        for t in (KV, QG):
            for j in range(2):
                pltpu.make_async_copy(
                    sources[t][j].at[:, columns(place, h)], rb.at[OWN, t, h, mine, j], load_sem.at[t, h]
                ).start()
        return carry

    lax.fori_loop(0, heads, load, 0)

    def row_copy(mate, t, h, j):
        kind, shard, there = mate
        return remote(
            sources[t][j].at[:, columns(real(shard), h)], rb.at[OWN, t, h, there, j],
            row_send.at[t, h, kind], row_recv.at[t, h, there], first + real(shard),
        )

    def row_pair(mate, t, h):
        kind, shard, _ = mate
        pair = rb.at[OWN, t, h, shard]
        return remote(pair, pair, row_send.at[t, h, kind], row_recv.at[t, h, shard], first + real(shard))

    def bias_copy(mate):
        kind, shard, there = mate
        src = bias.at[OWN, mine] if kind == 0 else turned
        return remote(src, bias.at[OWN, there], bias_send.at[kind], bias_recv.at[there], first + real(shard))

    def bias_arrival(mate):
        kind, shard, _ = mate
        tile = bias.at[OWN, shard]
        return remote(tile, tile, bias_send.at[kind], bias_recv.at[shard], first + real(shard))

    def zbias_copy(side, landing):
        return remote(packed.at[OWN], packed.at[landing], zbias_send.at[side], zbias_recv.at[landing], target[side])

    def z_copy(side, t, h, shard):
        return remote(
            rb.at[OWN, t, h, shard], rb.at[other[side], t, h, shard],
            z_send.at[side, t, h], z_recv.at[other[side], t, h, shard], target[side],
        )

    def z_arrival(side, t, h, shard):
        return remote(
            rb.at[OWN, t, h, shard], rb.at[side, t, h, shard],
            z_send.at[side, t, h], z_recv.at[side, t, h, shard], target[side],
        )

    def z_whole(side, t, h):
        return remote(
            rb.at[OWN, t, h], rb.at[side, t, h], z_send.at[side, t, h], z_recv.at[side, t, h, 0], target[side]
        )

    def stat_copy(side, landing, h):
        return remote(
            stats.at[OWN, h], stats.at[landing, h], stat_send.at[side, h], stat_recv.at[landing, h], target[side]
        )

    def exchange(mate, t, h):
        for j in range(2):
            row_copy(mate, t, h, j).start()

    def loaded(t, h):
        pair = rb.at[OWN, t, h, mine]
        pltpu.make_async_copy(pair, pair, load_sem.at[t, h]).wait()

    def row_arrived(t, h):
        loaded(t, h)
        for mate in mates:
            row_pair(mate, t, h).wait_recv()

    def z_items(t, h, items):
        def both(side):
            for i in items:
                z_copy(side, t, h, ORDER[side][i]).start()
        at_sides(both)

    def z_shard(t, h, shard):
        at_sides(lambda side: z_copy(side, t, h, shard).start())

    def give_back(j, h, shard):
        block = held.at[j, h, shard]
        cols = results[j].at[:, columns(place, h)]
        if shard >= 2:
            remote(block, cols, ret_send.at[h], ret_recv.at[3 - mine], first + real(shard)).start()
        else:
            @pl.when(mine == shard)
            def _():
                pltpu.make_async_copy(block, cols, own_sem.at[h]).start()

            @pl.when(mine != shard)
            def _():
                remote(block, cols, ret_send.at[h], ret_recv.at[mine], first + real(beside)).start()

    def stacked(t, h, j, places):
        return jnp.concatenate([rb[held_by[side], t, h, b, j] for side, b, _ in places], axis=0)

    def needs(t, h, places, ready):
        for side in (UP, DN):
            new = [b for s, b, _ in places if s == side and (s, b) not in ready]
            ready.update((side, b) for b in new)
            if new:
                @pl.when(exists[side])
                def _(side=side, new=new):
                    for b in new:
                        z_arrival(side, t, h, b).wait_recv()

    def query_side(h):
        lane = lax.broadcasted_iota(jnp.int32, (rows, 128), 1)
        table = jnp.zeros((rows, 128), jnp.float32)
        ready = set()
        for a in TURNS:
            places = readers(a, 1)
            needs(KV, h, places, ready)
            keys, values = stacked(KV, h, 0, places), stacked(KV, h, 1, places)
            queries, grads = rb[OWN, QG, h, a, 0], rb[OWN, QG, h, a, 1]
            shift = jnp.concatenate([bias[OWN, a, d:d + 1, :] for _, _, d in places], axis=1)
            scores = lax.dot_general(queries, keys, NT, preferred_element_type=jnp.float32)
            scores = scores * scale - shift
            top = jnp.max(scores, axis=1, keepdims=True)
            weights = jnp.exp(scores - top)
            total = jnp.sum(weights, axis=1, keepdims=True)
            exact = weights * (1.0 / total)
            out = jnp.dot(exact.astype(jnp.bfloat16), values, preferred_element_type=jnp.float32)
            out = out.astype(jnp.bfloat16)
            held[OUT, h, a] = out
            delta = jnp.sum(grads.astype(jnp.float32) * out.astype(jnp.float32), axis=1, keepdims=True)
            dprobs = lax.dot_general(grads, values, NT, preferred_element_type=jnp.float32)
            dscores = (exact * (dprobs - delta)).astype(jnp.bfloat16)
            grad = jnp.dot(dscores, keys, preferred_element_type=jnp.float32) * scale
            held[GQ, h, a] = grad.astype(jnp.bfloat16)
            table = jnp.where(lane == a, top + jnp.log(total), table)
            table = jnp.where(lane == a + ROW, delta, table)
            give_back(OUT, h, a)
            give_back(GQ, h, a)
        stats[OWN, h] = jnp.transpose(table)[:2 * ROW]
        at_sides(lambda side: stat_copy(side, other[side], h).start())

    def key_side(h):
        at_sides(lambda side: stat_copy(side, side, h).wait_recv())
        ready = set()
        partial = {}
        for b, part in KEY_PLAN:
            places = [place for place in readers(b, -1) if part == WHOLE or (place[:2] == LAST[b]) == (part == REST)]
            needs(QG, h, places, ready)
            queries, grads = stacked(QG, h, 0, places), stacked(QG, h, 1, places)
            keys, values = rb[OWN, KV, h, b, 0], rb[OWN, KV, h, b, 1]
            lse = jnp.concatenate(
                [stats[side, h, a:a + 1] + bias[side, a, d:d + 1] for side, a, d in places], axis=1
            )
            delta = jnp.concatenate([stats[side, h, a + ROW:a + ROW + 1] for side, a, _ in places], axis=1)
            scores = lax.dot_general(keys, queries, NT, preferred_element_type=jnp.float32)
            exact = jnp.exp(scores * scale - lse)
            value_grad = jnp.dot(exact.astype(jnp.bfloat16), grads, preferred_element_type=jnp.float32)
            if part == REST:
                value_grad = partial[b][0] + value_grad
            if part != START:
                held[GV, h, b] = value_grad.astype(jnp.bfloat16)
                give_back(GV, h, b)
            dprobs = lax.dot_general(values, grads, NT, preferred_element_type=jnp.float32)
            dscores = (exact * (dprobs - delta)).astype(jnp.bfloat16)
            key_grad = jnp.dot(dscores, queries, preferred_element_type=jnp.float32)
            if part == START:
                partial[b] = value_grad, key_grad
                continue
            if part == REST:
                key_grad = partial[b][1] + key_grad
            held[GK, h, b] = (key_grad * scale).astype(jnp.bfloat16)
            give_back(GK, h, b)

    pl.semaphore_wait(barrier, 3 + sum(jnp.where(exists[side], 1, 0) for side in (UP, DN)))

    for h in range(2):
        loaded(KV, h)
        z_shard(KV, h, mine)
    for t, h in ((KV, 0), (KV, 1), (QG, 0)):
        for mate in mates:
            exchange(mate, t, h)

    pltpu.make_async_copy(mask_hbm, mask_ref, mask_sem).wait()
    index = lax.broadcasted_iota(jnp.int32, (8, 128), 0)
    straight = jnp.zeros((8, 128), jnp.float32)
    mirrored = straight
    for d in range(7):
        straight = jnp.where(index == d, (1.0 - mask_ref[d].astype(jnp.float32)) * BIG, straight)
        mirrored = jnp.where(index == d, (1.0 - mask_ref[MIRROR[d]].astype(jnp.float32)) * BIG, mirrored)
    bias[OWN, mine] = jnp.where(flip == 0, straight, mirrored)
    turned[...] = jnp.where(flip == 0, mirrored, straight)

    for mate in mates:
        bias_copy(mate).start()
    for h in range(2):
        row_pair(mates[0], KV, h).wait_recv()
        z_shard(KV, h, beside)

    def exchange_rest(h, carry):
        @pl.when(h < heads)
        def _():
            for mate in mates:
                exchange(mate, KV, h)
        for mate in mates:
            exchange(mate, QG, h - 1)
        return carry

    lax.fori_loop(2, heads + 1, exchange_rest, 0)

    for side in (UP, DN):
        @pl.when(jnp.logical_not(exists[side]))
        def _(side=side):
            stats[side] = jnp.zeros(stats.shape[1:], jnp.float32)
            bias[side] = jnp.full(bias.shape[1:], BIG, jnp.float32)

    for h in range(2):
        for mate in mates[1:]:
            row_pair(mate, KV, h).wait_recv()
            z_shard(KV, h, mate[1])
    row_arrived(QG, 0)
    z_items(QG, 0, (0, 1, 2, 3))
    for mate in mates:
        bias_arrival(mate).wait_recv()
    column = lax.broadcasted_iota(jnp.int32, (8, 128), 1)
    packed[OWN] = functools.reduce(lambda tile, a: jnp.where(column == a, bias[OWN, a], tile), range(1, ROW), bias[OWN, 0])
    at_sides(lambda side: zbias_copy(side, other[side]).start())

    def step(i, carry):
        @pl.when(jnp.logical_and(i >= 1, i + 1 < heads))
        def _():
            row_arrived(KV, i + 1)
            z_items(KV, i + 1, (0, 1, 2, 3))

        @pl.when(jnp.logical_and(i >= 1, i < heads))
        def _():
            row_arrived(QG, i)

        @pl.when(i < heads)
        def _():
            query_side(i)

        @pl.when(jnp.logical_and(i >= 1, i < heads))
        def _():
            z_items(QG, i, (0, 1, 2, 3))

        @pl.when(i == 1)
        def _():
            at_sides(unpack)

        @pl.when(i >= 1)
        def _():
            drain_early(i - 1)
            key_side(i - 1)

        return carry

    def unpack(side):
        zbias_copy(side, side).wait_recv()
        for a in range(ROW):
            bias[side, a] = jnp.broadcast_to(packed[side][:, a:a + 1], (8, 128))

    def drain_early(h):
        for t in (KV, QG):
            for mate in mates:
                row_pair(mate, t, h).wait_send()

        def sent(side):
            z_whole(side, KV, h).wait_send()
            stat_copy(side, other[side], h).wait_send()

        at_sides(sent)

    lax.fori_loop(0, heads + 1, step, 0)

    for mate in mates:
        bias_copy(mate).wait_send()
    at_sides(lambda side: zbias_copy(side, other[side]).wait_send())

    def drain(h, carry):
        at_sides(lambda side: z_whole(side, QG, h).wait_send())
        blocks = held.at[pl.ds(0, 3), h]
        remote(blocks, blocks, ret_send.at[h], ret_recv.at[0], first + real(2)).wait_send()
        four = held.at[:, h, 0]
        pltpu.make_async_copy(four, four, own_sem.at[h]).wait()
        return carry

    lax.fori_loop(0, heads, drain, 0)

    for _, shard, _ in mates:
        block = held.at[0]
        remote(block, block, ret_send.at[0], ret_recv.at[shard], first + real(shard)).wait_recv()


def copy_out(*refs):
    sems = refs[8]
    copies = [pltpu.make_async_copy(refs[j], refs[4 + j], sems.at[j]) for j in range(4)]
    for copy in copies:
        copy.start()
    for copy in copies:
        copy.wait()


def finish(*arrays):
    return pl.pallas_call(
        copy_out,
        name="finish",
        out_shape=tuple(jax.ShapeDtypeStruct(a.shape, a.dtype) for a in arrays),
        in_specs=[pl.BlockSpec(memory_space=pl.ANY)] * 4,
        out_specs=(pl.BlockSpec(memory_space=pltpu.HBM),) * 4,
        scratch_shapes=[pltpu.SemaphoreType.DMA((4,))],
        compiler_params=pltpu.CompilerParams(vmem_limit_bytes=1 << 20),
    )(*arrays)


def local(seq, query, key, value, grad_out, tile_mask):
    rows, features = query.shape
    heads = features // HEAD // ROW
    pairs = rows * rows * features * 7
    dma = pltpu.SemaphoreType.DMA
    results = pl.pallas_call(
        functools.partial(kernel, seq),
        name="radial",
        out_shape=(jax.ShapeDtypeStruct((rows, features), jnp.bfloat16),) * 4,
        in_specs=[pl.BlockSpec(memory_space=pltpu.HBM)] + [pl.BlockSpec(memory_space=pltpu.HBM)] * 4,
        out_specs=(pl.BlockSpec(memory_space=pl.ANY),) * 4,
        scratch_shapes=[
            pltpu.SMEM((7,), jnp.int32),
            dma(()),
            pltpu.VMEM((3, 2, heads, ROW, 2, rows, HEAD), jnp.bfloat16),
            pltpu.VMEM((4, heads, ROW, rows, HEAD), jnp.bfloat16),
            pltpu.VMEM((3, ROW, 8, 128), jnp.float32),
            pltpu.VMEM((8, 128), jnp.float32),
            pltpu.VMEM((3, 8, 128), jnp.float32),
            pltpu.VMEM((3, heads, 8, 128), jnp.float32),
            dma((2, heads)),
            dma((2, heads, 3)), dma((2, heads, ROW)),
            dma((3, 2, heads)), dma((3, 2, heads, ROW)),
            dma((3,)), dma((ROW,)), dma((3,)), dma((3,)),
            dma((3, heads)), dma((3, heads)),
            dma((heads,)), dma((heads,)), dma((ROW,)),
        ],
        compiler_params=pltpu.CompilerParams(
            collective_id=0, has_side_effects=True, vmem_limit_bytes=32 << 20
        ),
        cost_estimate=pl.CostEstimate(
            flops=16 * pairs, transcendentals=2 * pairs // HEAD, bytes_accessed=16 * rows * features
        ),
    )(*(pltpu.with_memory_space_constraint(a, pltpu.HBM) for a in (tile_mask.reshape(7), query, key, value, grad_out)))
    return tuple(finish(*results))


def solution(mesh):
    spec = P(("grp", "seq"), None)
    return jax.shard_map(
        functools.partial(local, mesh.shape["seq"]),
        mesh=mesh,
        in_specs=(spec,) * 4 + (P("seq", None, None, None),),
        out_specs=(spec,) * 4,
        check_vma=False,
    )
```

```python
import functools

import jax
import jax.numpy as jnp
from jax import lax
from jax.experimental import pallas as pl
from jax.experimental.pallas import tpu as pltpu
from jax.sharding import PartitionSpec as P

HEAD = 128
ROW = 4
BIG = 1e30
DIST = {0: 0, 1: 1, -1: 2, 2: 3, -2: 4, 4: 5, -4: 6}

OWN, UP, DN = range(3)
KV, QG = range(2)
OUT, GQ, GK, GV = range(4)
SHIFT = {OWN: 0, UP: ROW, DN: -ROW}
NT = (((1,), (1,)), ((), ()))


def readers(a, sign):
    found = []
    for side in (OWN, UP, DN):
        for b in range(ROW):
            offset = sign * (SHIFT[side] + b - a)
            if offset in DIST:
                found.append((side, b, DIST[offset]))
    return found


ORDER = {UP: (2, 3, 0, 1), DN: (0, 1, 3, 2)}
TURNS = (0, 3, 2, 1)
WHOLE, START, REST = range(3)
LAST = {2: (UP, 2), 3: (UP, 3)}
KEY_PLAN = ((2, START), (3, START), (3, REST), (0, WHOLE), (2, REST), (1, WHOLE))
MIRROR = (0, 2, 1, 4, 3, 6, 5)


def kernel(seq, mask_hbm, q_ref, k_ref, v_ref, g_ref, att_ref, gq_ref, gk_ref, gv_ref,
           mask_ref, mask_sem, ready, rb, held, bias, turned, packed, stats,
           load_sem, row_send, row_recv, z_send, z_recv, bias_send, bias_recv, zbias_send, zbias_recv,
           stat_send, stat_recv, own_sem, ret_send, ret_recv):
    rows = q_ref.shape[0]
    heads = q_ref.shape[1] // HEAD // ROW
    scale = HEAD ** (-0.5)
    sources = ((k_ref, v_ref), (q_ref, g_ref))
    results = (att_ref, gq_ref, gk_ref, gv_ref)

    me = lax.axis_index("seq")
    place = lax.rem(me, ROW)
    first = me - place
    flip = lax.div(place, 2)

    def real(shard):
        return shard + flip * (3 - 2 * shard)

    mine = real(place)
    beside = 1 - mine
    mates = ((0, beside, mine), (1, 2, 3 - mine), (2, 3, 3 - mine))
    target = {UP: me + ROW * (1 - 2 * flip), DN: me - ROW * (1 - 2 * flip)}
    exists = {side: jnp.logical_and(target[side] >= 0, target[side] < seq) for side in (UP, DN)}
    other = {UP: DN, DN: UP}
    held_by = {OWN: OWN, **{side: jnp.where(exists[side], side, OWN) for side in (UP, DN)}}

    def remote(src, dst, send, recv, device):
        return pltpu.make_async_remote_copy(
            src_ref=src, dst_ref=dst, send_sem=send, recv_sem=recv,
            device_id={"seq": device}, device_id_type=pl.DeviceIdType.MESH,
        )

    def at_sides(action):
        for side in (UP, DN):
            @pl.when(exists[side])
            def _(side=side):
                action(side)

    def columns(part, h):
        return pl.ds(pl.multiple_of((part * heads + h) * HEAD, HEAD), HEAD)

    pltpu.make_async_copy(mask_hbm, mask_ref, mask_sem).start()
    barrier = pltpu.get_barrier_semaphore()
    for _, shard, _ in mates:
        pl.semaphore_signal(barrier, inc=1, device_id={"seq": first + real(shard)})
    @pl.when(me + ROW < seq)
    def _():
        pl.semaphore_signal(barrier, inc=1, device_id={"seq": me + ROW})


    def load(h, carry):
        for t in (KV, QG):
            for j in range(2):
                pltpu.make_async_copy(
                    sources[t][j].at[:, columns(place, h)], rb.at[OWN, t, h, mine, j], load_sem.at[t, h]
                ).start()
        return carry

    lax.fori_loop(0, heads, load, 0)

    def row_copy(mate, t, h, j):
        kind, shard, there = mate
        return remote(
            sources[t][j].at[:, columns(real(shard), h)], rb.at[OWN, t, h, there, j],
            row_send.at[t, h, kind], row_recv.at[t, h, there], first + real(shard),
        )

    def row_pair(mate, t, h):
        kind, shard, _ = mate
        pair = rb.at[OWN, t, h, shard]
        return remote(pair, pair, row_send.at[t, h, kind], row_recv.at[t, h, shard], first + real(shard))

    def bias_copy(mate):
        kind, shard, there = mate
        src = bias.at[OWN, mine] if kind == 0 else turned
        return remote(src, bias.at[OWN, there], bias_send.at[kind], bias_recv.at[there], first + real(shard))

    def bias_arrival(mate):
        kind, shard, _ = mate
        tile = bias.at[OWN, shard]
        return remote(tile, tile, bias_send.at[kind], bias_recv.at[shard], first + real(shard))

    def zbias_copy(side, landing):
        return remote(packed.at[OWN], packed.at[landing], zbias_send.at[side], zbias_recv.at[landing], target[side])

    def z_copy(side, t, h, shard):
        return remote(
            rb.at[OWN, t, h, shard], rb.at[other[side], t, h, shard],
            z_send.at[side, t, h], z_recv.at[other[side], t, h, shard], target[side],
        )

    def z_arrival(side, t, h, shard):
        return remote(
            rb.at[OWN, t, h, shard], rb.at[side, t, h, shard],
            z_send.at[side, t, h], z_recv.at[side, t, h, shard], target[side],
        )

    def z_whole(side, t, h):
        return remote(
            rb.at[OWN, t, h], rb.at[side, t, h], z_send.at[side, t, h], z_recv.at[side, t, h, 0], target[side]
        )

    def stat_copy(side, landing, h):
        return remote(
            stats.at[OWN, h], stats.at[landing, h], stat_send.at[side, h], stat_recv.at[landing, h], target[side]
        )

    def exchange(mate, t, h):
        for j in range(2):
            row_copy(mate, t, h, j).start()

    def loaded(t, h):
        pair = rb.at[OWN, t, h, mine]
        pltpu.make_async_copy(pair, pair, load_sem.at[t, h]).wait()

    def row_arrived(t, h):
        loaded(t, h)
        for mate in mates:
            row_pair(mate, t, h).wait_recv()

    def z_items(t, h, items):
        def both(side):
            for i in items:
                z_copy(side, t, h, ORDER[side][i]).start()
        at_sides(both)

    def z_shard(t, h, shard):
        at_sides(lambda side: z_copy(side, t, h, shard).start())

    def give_back(j, h, shard):
        block = held.at[j, h, shard]
        cols = results[j].at[:, columns(place, h)]
        if shard >= 2:
            remote(block, cols, ret_send.at[h], ret_recv.at[3 - mine], first + real(shard)).start()
        else:
            @pl.when(mine == shard)
            def _():
                pltpu.make_async_copy(block, cols, own_sem.at[h]).start()

            @pl.when(mine != shard)
            def _():
                remote(block, cols, ret_send.at[h], ret_recv.at[mine], first + real(beside)).start()

    def stacked(t, h, j, places):
        return jnp.concatenate([rb[held_by[side], t, h, b, j] for side, b, _ in places], axis=0)

    def needs(t, h, places, ready):
        for side in (UP, DN):
            new = [b for s, b, _ in places if s == side and (s, b) not in ready]
            ready.update((side, b) for b in new)
            if new:
                @pl.when(exists[side])
                def _(side=side, new=new):
                    for b in new:
                        z_arrival(side, t, h, b).wait_recv()

    def query_side(h):
        lane = lax.broadcasted_iota(jnp.int32, (rows, 128), 1)
        table = jnp.zeros((rows, 128), jnp.float32)
        ready = set()
        for a in TURNS:
            places = readers(a, 1)
            needs(KV, h, places, ready)
            keys, values = stacked(KV, h, 0, places), stacked(KV, h, 1, places)
            queries, grads = rb[OWN, QG, h, a, 0], rb[OWN, QG, h, a, 1]
            shift = jnp.concatenate([bias[OWN, a, d:d + 1, :] for _, _, d in places], axis=1)
            scores = lax.dot_general(queries, keys, NT, preferred_element_type=jnp.float32)
            scores = scores * scale - shift
            top = jnp.max(scores, axis=1, keepdims=True)
            weights = jnp.exp(scores - top)
            total = jnp.sum(weights, axis=1, keepdims=True)
            exact = weights * (1.0 / total)
            out = jnp.dot(exact.astype(jnp.bfloat16), values, preferred_element_type=jnp.float32)
            out = out.astype(jnp.bfloat16)
            held[OUT, h, a] = out
            delta = jnp.sum(grads.astype(jnp.float32) * out.astype(jnp.float32), axis=1, keepdims=True)
            dprobs = lax.dot_general(grads, values, NT, preferred_element_type=jnp.float32)
            dscores = (exact * (dprobs - delta)).astype(jnp.bfloat16)
            grad = jnp.dot(dscores, keys, preferred_element_type=jnp.float32) * scale
            held[GQ, h, a] = grad.astype(jnp.bfloat16)
            table = jnp.where(lane == a, top + jnp.log(total), table)
            table = jnp.where(lane == a + ROW, delta, table)
            give_back(OUT, h, a)
            give_back(GQ, h, a)
        stats[OWN, h] = jnp.transpose(table)[:2 * ROW]
        at_sides(lambda side: stat_copy(side, other[side], h).start())

    def key_side(h):
        at_sides(lambda side: stat_copy(side, side, h).wait_recv())
        ready = set()
        partial = {}
        for b, part in KEY_PLAN:
            places = [place for place in readers(b, -1) if part == WHOLE or (place[:2] == LAST[b]) == (part == REST)]
            needs(QG, h, places, ready)
            queries, grads = stacked(QG, h, 0, places), stacked(QG, h, 1, places)
            keys, values = rb[OWN, KV, h, b, 0], rb[OWN, KV, h, b, 1]
            lse = jnp.concatenate(
                [stats[side, h, a:a + 1] + bias[side, a, d:d + 1] for side, a, d in places], axis=1
            )
            delta = jnp.concatenate([stats[side, h, a + ROW:a + ROW + 1] for side, a, _ in places], axis=1)
            scores = lax.dot_general(keys, queries, NT, preferred_element_type=jnp.float32)
            exact = jnp.exp(scores * scale - lse)
            value_grad = jnp.dot(exact.astype(jnp.bfloat16), grads, preferred_element_type=jnp.float32)
            if part == REST:
                value_grad = partial[b][0] + value_grad
            if part != START:
                held[GV, h, b] = value_grad.astype(jnp.bfloat16)
                give_back(GV, h, b)
            dprobs = lax.dot_general(values, grads, NT, preferred_element_type=jnp.float32)
            dscores = (exact * (dprobs - delta)).astype(jnp.bfloat16)
            key_grad = jnp.dot(dscores, queries, preferred_element_type=jnp.float32)
            if part == START:
                partial[b] = value_grad, key_grad
                continue
            if part == REST:
                key_grad = partial[b][1] + key_grad
            held[GK, h, b] = (key_grad * scale).astype(jnp.bfloat16)
            give_back(GK, h, b)

    pl.semaphore_wait(barrier, 3 + jnp.where(me >= ROW, 1, 0))

    @pl.when(me >= ROW)
    def _():
        pl.semaphore_signal(ready, inc=1, device_id={"seq": me - ROW})


    for h in range(2):
        loaded(KV, h)
        for side in (UP, DN):
            @pl.when(jnp.logical_and(exists[side], target[side] < me))
            def _(side=side, h=h):
                z_copy(side, KV, h, mine).start()

    for t, h in ((KV, 0), (KV, 1), (QG, 0)):
        for mate in mates:
            exchange(mate, t, h)

    @pl.when(me + ROW < seq)
    def _():
        pl.semaphore_wait(ready, 1)

    for h in range(2):
        for side in (UP, DN):
            @pl.when(jnp.logical_and(exists[side], target[side] > me))
            def _(side=side, h=h):
                z_copy(side, KV, h, mine).start()


    pltpu.make_async_copy(mask_hbm, mask_ref, mask_sem).wait()
    index = lax.broadcasted_iota(jnp.int32, (8, 128), 0)
    straight = jnp.zeros((8, 128), jnp.float32)
    mirrored = straight
    for d in range(7):
        straight = jnp.where(index == d, (1.0 - mask_ref[d].astype(jnp.float32)) * BIG, straight)
        mirrored = jnp.where(index == d, (1.0 - mask_ref[MIRROR[d]].astype(jnp.float32)) * BIG, mirrored)
    bias[OWN, mine] = jnp.where(flip == 0, straight, mirrored)
    turned[...] = jnp.where(flip == 0, mirrored, straight)

    for mate in mates:
        bias_copy(mate).start()
    for h in range(2):
        row_pair(mates[0], KV, h).wait_recv()
        z_shard(KV, h, beside)

    def exchange_rest(h, carry):
        @pl.when(h < heads)
        def _():
            for mate in mates:
                exchange(mate, KV, h)
        for mate in mates:
            exchange(mate, QG, h - 1)
        return carry

    lax.fori_loop(2, heads + 1, exchange_rest, 0)

    for side in (UP, DN):
        @pl.when(jnp.logical_not(exists[side]))
        def _(side=side):
            stats[side] = jnp.zeros(stats.shape[1:], jnp.float32)
            bias[side] = jnp.full(bias.shape[1:], BIG, jnp.float32)

    for h in range(2):
        for mate in mates[1:]:
            row_pair(mate, KV, h).wait_recv()
            z_shard(KV, h, mate[1])
    row_arrived(QG, 0)
    z_items(QG, 0, (0, 1, 2, 3))
    for mate in mates:
        bias_arrival(mate).wait_recv()
    column = lax.broadcasted_iota(jnp.int32, (8, 128), 1)
    packed[OWN] = functools.reduce(lambda tile, a: jnp.where(column == a, bias[OWN, a], tile), range(1, ROW), bias[OWN, 0])
    at_sides(lambda side: zbias_copy(side, other[side]).start())

    def step(i, carry):
        @pl.when(jnp.logical_and(i >= 1, i + 1 < heads))
        def _():
            row_arrived(KV, i + 1)
            z_items(KV, i + 1, (0, 1, 2, 3))

        @pl.when(jnp.logical_and(i >= 1, i < heads))
        def _():
            row_arrived(QG, i)

        @pl.when(i < heads)
        def _():
            query_side(i)

        @pl.when(jnp.logical_and(i >= 1, i < heads))
        def _():
            z_items(QG, i, (0, 1, 2, 3))

        @pl.when(i == 1)
        def _():
            at_sides(unpack)

        @pl.when(i >= 1)
        def _():
            drain_early(i - 1)
            key_side(i - 1)

        return carry

    def unpack(side):
        zbias_copy(side, side).wait_recv()
        for a in range(ROW):
            bias[side, a] = jnp.broadcast_to(packed[side][:, a:a + 1], (8, 128))

    def drain_early(h):
        for t in (KV, QG):
            for mate in mates:
                row_pair(mate, t, h).wait_send()

        def sent(side):
            z_whole(side, KV, h).wait_send()
            stat_copy(side, other[side], h).wait_send()

        at_sides(sent)

    lax.fori_loop(0, heads + 1, step, 0)

    for mate in mates:
        bias_copy(mate).wait_send()
    at_sides(lambda side: zbias_copy(side, other[side]).wait_send())

    def drain(h, carry):
        at_sides(lambda side: z_whole(side, QG, h).wait_send())
        blocks = held.at[pl.ds(0, 3), h]
        remote(blocks, blocks, ret_send.at[h], ret_recv.at[0], first + real(2)).wait_send()
        four = held.at[:, h, 0]
        pltpu.make_async_copy(four, four, own_sem.at[h]).wait()
        return carry

    lax.fori_loop(0, heads, drain, 0)

    for _, shard, _ in mates:
        block = held.at[0]
        remote(block, block, ret_send.at[0], ret_recv.at[shard], first + real(shard)).wait_recv()


def copy_out(*refs):
    sems = refs[8]
    copies = [pltpu.make_async_copy(refs[j], refs[4 + j], sems.at[j]) for j in range(4)]
    for copy in copies:
        copy.start()
    for copy in copies:
        copy.wait()


def finish(*arrays):
    return pl.pallas_call(
        copy_out,
        name="finish",
        out_shape=tuple(jax.ShapeDtypeStruct(a.shape, a.dtype) for a in arrays),
        in_specs=[pl.BlockSpec(memory_space=pl.ANY)] * 4,
        out_specs=(pl.BlockSpec(memory_space=pltpu.HBM),) * 4,
        scratch_shapes=[pltpu.SemaphoreType.DMA((4,))],
        compiler_params=pltpu.CompilerParams(vmem_limit_bytes=1 << 20),
    )(*arrays)


def local(seq, query, key, value, grad_out, tile_mask):
    rows, features = query.shape
    heads = features // HEAD // ROW
    pairs = rows * rows * features * 7
    dma = pltpu.SemaphoreType.DMA
    results = pl.pallas_call(
        functools.partial(kernel, seq),
        name="radial",
        out_shape=(jax.ShapeDtypeStruct((rows, features), jnp.bfloat16),) * 4,
        in_specs=[pl.BlockSpec(memory_space=pltpu.HBM)] + [pl.BlockSpec(memory_space=pltpu.HBM)] * 4,
        out_specs=(pl.BlockSpec(memory_space=pl.ANY),) * 4,
        scratch_shapes=[
            pltpu.SMEM((7,), jnp.int32),
            dma(()),
            pltpu.SemaphoreType.REGULAR,
            pltpu.VMEM((3, 2, heads, ROW, 2, rows, HEAD), jnp.bfloat16),
            pltpu.VMEM((4, heads, ROW, rows, HEAD), jnp.bfloat16),
            pltpu.VMEM((3, ROW, 8, 128), jnp.float32),
            pltpu.VMEM((8, 128), jnp.float32),
            pltpu.VMEM((3, 8, 128), jnp.float32),
            pltpu.VMEM((3, heads, 8, 128), jnp.float32),
            dma((2, heads)),
            dma((2, heads, 3)), dma((2, heads, ROW)),
            dma((3, 2, heads)), dma((3, 2, heads, ROW)),
            dma((3,)), dma((ROW,)), dma((3,)), dma((3,)),
            dma((3, heads)), dma((3, heads)),
            dma((heads,)), dma((heads,)), dma((ROW,)),
        ],
        compiler_params=pltpu.CompilerParams(
            collective_id=0, has_side_effects=True, vmem_limit_bytes=32 << 20
        ),
        cost_estimate=pl.CostEstimate(
            flops=16 * pairs, transcendentals=2 * pairs // HEAD, bytes_accessed=16 * rows * features
        ),
    )(*(pltpu.with_memory_space_constraint(a, pltpu.HBM) for a in (tile_mask.reshape(7), query, key, value, grad_out)))
    return tuple(finish(*results))


def solution(mesh):
    spec = P(("grp", "seq"), None)
    return jax.shard_map(
        functools.partial(local, mesh.shape["seq"]),
        mesh=mesh,
        in_specs=(spec,) * 4 + (P("seq", None, None, None),),
        out_specs=(spec,) * 4,
        check_vma=False,
    )
```

```python
import functools

import jax
import jax.numpy as jnp
from jax import lax
from jax.experimental import pallas as pl
from jax.experimental.pallas import tpu as pltpu
from jax.sharding import PartitionSpec as P

HEAD = 128
ROW = 4
BIG = 1e30
DIST = {0: 0, 1: 1, -1: 2, 2: 3, -2: 4, 4: 5, -4: 6}

OWN, UP, DN = range(3)
KV, QG = range(2)
OUT, GQ, GK, GV = range(4)
SHIFT = {OWN: 0, UP: ROW, DN: -ROW}
NT = (((1,), (1,)), ((), ()))


def readers(a, sign):
    found = []
    for side in (OWN, UP, DN):
        for b in range(ROW):
            offset = sign * (SHIFT[side] + b - a)
            if offset in DIST:
                found.append((side, b, DIST[offset]))
    return found


ORDER = {UP: (2, 3, 0, 1), DN: (0, 1, 3, 2)}
TURNS = (0, 3, 2, 1)
WHOLE, START, REST = range(3)
LAST = {1: (DN, 1), 2: (UP, 2), 3: (UP, 3)}
KEY_PLAN = ((2, START), (3, START), (1, START), (3, REST), (0, WHOLE), (2, REST), (1, REST))
MIRROR = (0, 2, 1, 4, 3, 6, 5)


def kernel(seq, mask_hbm, q_ref, k_ref, v_ref, g_ref, att_ref, gq_ref, gk_ref, gv_ref,
           mask_ref, mask_sem, rb, held, bias, turned, packed, stats,
           load_sem, row_send, row_recv, z_send, z_recv, bias_send, bias_recv, zbias_send, zbias_recv,
           stat_send, stat_recv, own_sem, ret_send, ret_recv):
    rows = q_ref.shape[0]
    heads = q_ref.shape[1] // HEAD // ROW
    scale = HEAD ** (-0.5)
    sources = ((k_ref, v_ref), (q_ref, g_ref))
    results = (att_ref, gq_ref, gk_ref, gv_ref)

    me = lax.axis_index("seq")
    place = lax.rem(me, ROW)
    first = me - place
    flip = lax.div(place, 2)

    def real(shard):
        return shard + flip * (3 - 2 * shard)

    mine = real(place)
    beside = 1 - mine
    mates = ((0, beside, mine), (1, 2, 3 - mine), (2, 3, 3 - mine))
    target = {UP: me + ROW * (1 - 2 * flip), DN: me - ROW * (1 - 2 * flip)}
    exists = {side: jnp.logical_and(target[side] >= 0, target[side] < seq) for side in (UP, DN)}
    other = {UP: DN, DN: UP}
    held_by = {OWN: OWN, **{side: jnp.where(exists[side], side, OWN) for side in (UP, DN)}}

    def remote(src, dst, send, recv, device):
        return pltpu.make_async_remote_copy(
            src_ref=src, dst_ref=dst, send_sem=send, recv_sem=recv,
            device_id={"seq": device}, device_id_type=pl.DeviceIdType.MESH,
        )

    def at_sides(action):
        for side in (UP, DN):
            @pl.when(exists[side])
            def _(side=side):
                action(side)

    def columns(part, h):
        return pl.ds(pl.multiple_of((part * heads + h) * HEAD, HEAD), HEAD)

    pltpu.make_async_copy(mask_hbm, mask_ref, mask_sem).start()
    barrier = pltpu.get_barrier_semaphore()
    for _, shard, _ in mates:
        pl.semaphore_signal(barrier, inc=1, device_id={"seq": first + real(shard)})
    at_sides(lambda side: pl.semaphore_signal(barrier, inc=1, device_id={"seq": target[side]}))

    def load(h, carry):
        for t in (KV, QG):
            for j in range(2):
                pltpu.make_async_copy(
                    sources[t][j].at[:, columns(place, h)], rb.at[OWN, t, h, mine, j], load_sem.at[t, h]
                ).start()
        return carry

    lax.fori_loop(0, heads, load, 0)

    def row_copy(mate, t, h, j):
        kind, shard, there = mate
        return remote(
            sources[t][j].at[:, columns(real(shard), h)], rb.at[OWN, t, h, there, j],
            row_send.at[t, h, kind], row_recv.at[t, h, there], first + real(shard),
        )

    def row_pair(mate, t, h):
        kind, shard, _ = mate
        pair = rb.at[OWN, t, h, shard]
        return remote(pair, pair, row_send.at[t, h, kind], row_recv.at[t, h, shard], first + real(shard))

    def bias_copy(mate):
        kind, shard, there = mate
        src = bias.at[OWN, mine] if kind == 0 else turned
        return remote(src, bias.at[OWN, there], bias_send.at[kind], bias_recv.at[there], first + real(shard))

    def bias_arrival(mate):
        kind, shard, _ = mate
        tile = bias.at[OWN, shard]
        return remote(tile, tile, bias_send.at[kind], bias_recv.at[shard], first + real(shard))

    def zbias_copy(side, landing):
        return remote(packed.at[OWN], packed.at[landing], zbias_send.at[side], zbias_recv.at[landing], target[side])

    def z_copy(side, t, h, shard):
        return remote(
            rb.at[OWN, t, h, shard], rb.at[other[side], t, h, shard],
            z_send.at[side, t, h], z_recv.at[other[side], t, h, shard], target[side],
        )

    def z_arrival(side, t, h, shard):
        return remote(
            rb.at[OWN, t, h, shard], rb.at[side, t, h, shard],
            z_send.at[side, t, h], z_recv.at[side, t, h, shard], target[side],
        )

    def z_whole(side, t, h):
        return remote(
            rb.at[OWN, t, h], rb.at[side, t, h], z_send.at[side, t, h], z_recv.at[side, t, h, 0], target[side]
        )

    def stat_copy(side, landing, h):
        return remote(
            stats.at[OWN, h], stats.at[landing, h], stat_send.at[side, h], stat_recv.at[landing, h], target[side]
        )

    def exchange(mate, t, h):
        for j in range(2):
            row_copy(mate, t, h, j).start()

    def loaded(t, h):
        pair = rb.at[OWN, t, h, mine]
        pltpu.make_async_copy(pair, pair, load_sem.at[t, h]).wait()

    def row_arrived(t, h):
        loaded(t, h)
        for mate in mates:
            row_pair(mate, t, h).wait_recv()

    def z_items(t, h, items):
        def both(side):
            for i in items:
                z_copy(side, t, h, ORDER[side][i]).start()
        at_sides(both)

    def z_shard(t, h, shard):
        at_sides(lambda side: z_copy(side, t, h, shard).start())

    def give_back(j, h, shard):
        block = held.at[j, h, shard]
        cols = results[j].at[:, columns(place, h)]
        if shard >= 2:
            remote(block, cols, ret_send.at[h], ret_recv.at[3 - mine], first + real(shard)).start()
        else:
            @pl.when(mine == shard)
            def _():
                pltpu.make_async_copy(block, cols, own_sem.at[h]).start()

            @pl.when(mine != shard)
            def _():
                remote(block, cols, ret_send.at[h], ret_recv.at[mine], first + real(beside)).start()

    def stacked(t, h, j, places):
        return jnp.concatenate([rb[held_by[side], t, h, b, j] for side, b, _ in places], axis=0)

    def needs(t, h, places, ready):
        for side in (UP, DN):
            new = [b for s, b, _ in places if s == side and (s, b) not in ready]
            ready.update((side, b) for b in new)
            if new:
                @pl.when(exists[side])
                def _(side=side, new=new):
                    for b in new:
                        z_arrival(side, t, h, b).wait_recv()

    def query_side(h):
        lane = lax.broadcasted_iota(jnp.int32, (rows, 128), 1)
        table = jnp.zeros((rows, 128), jnp.float32)
        ready = set()
        for a in TURNS:
            places = readers(a, 1)
            needs(KV, h, places, ready)
            keys, values = stacked(KV, h, 0, places), stacked(KV, h, 1, places)
            queries, grads = rb[OWN, QG, h, a, 0], rb[OWN, QG, h, a, 1]
            shift = jnp.concatenate([bias[OWN, a, d:d + 1, :] for _, _, d in places], axis=1)
            scores = lax.dot_general(queries, keys, NT, preferred_element_type=jnp.float32)
            scores = scores * scale - shift
            top = jnp.max(scores, axis=1, keepdims=True)
            weights = jnp.exp(scores - top)
            total = jnp.sum(weights, axis=1, keepdims=True)
            exact = weights * (1.0 / total)
            out = jnp.dot(exact.astype(jnp.bfloat16), values, preferred_element_type=jnp.float32)
            out = out.astype(jnp.bfloat16)
            held[OUT, h, a] = out
            delta = jnp.sum(grads.astype(jnp.float32) * out.astype(jnp.float32), axis=1, keepdims=True)
            dprobs = lax.dot_general(grads, values, NT, preferred_element_type=jnp.float32)
            dscores = (exact * (dprobs - delta)).astype(jnp.bfloat16)
            grad = jnp.dot(dscores, keys, preferred_element_type=jnp.float32) * scale
            held[GQ, h, a] = grad.astype(jnp.bfloat16)
            table = jnp.where(lane == a, top + jnp.log(total), table)
            table = jnp.where(lane == a + ROW, delta, table)
            give_back(OUT, h, a)
            give_back(GQ, h, a)
        stats[OWN, h] = jnp.transpose(table)[:2 * ROW]
        at_sides(lambda side: stat_copy(side, other[side], h).start())

    def key_side(h):
        at_sides(lambda side: stat_copy(side, side, h).wait_recv())
        ready = set()
        partial = {}
        for b, part in KEY_PLAN:
            places = [place for place in readers(b, -1) if part == WHOLE or (place[:2] == LAST[b]) == (part == REST)]
            needs(QG, h, places, ready)
            queries, grads = stacked(QG, h, 0, places), stacked(QG, h, 1, places)
            keys, values = rb[OWN, KV, h, b, 0], rb[OWN, KV, h, b, 1]
            lse = jnp.concatenate(
                [stats[side, h, a:a + 1] + bias[side, a, d:d + 1] for side, a, d in places], axis=1
            )
            delta = jnp.concatenate([stats[side, h, a + ROW:a + ROW + 1] for side, a, _ in places], axis=1)
            scores = lax.dot_general(keys, queries, NT, preferred_element_type=jnp.float32)
            exact = jnp.exp(scores * scale - lse)
            value_grad = jnp.dot(exact.astype(jnp.bfloat16), grads, preferred_element_type=jnp.float32)
            if part == REST:
                value_grad = partial[b][0] + value_grad
            if part != START:
                held[GV, h, b] = value_grad.astype(jnp.bfloat16)
                give_back(GV, h, b)
            dprobs = lax.dot_general(values, grads, NT, preferred_element_type=jnp.float32)
            dscores = (exact * (dprobs - delta)).astype(jnp.bfloat16)
            key_grad = jnp.dot(dscores, queries, preferred_element_type=jnp.float32)
            if part == START:
                partial[b] = value_grad, key_grad
                continue
            if part == REST:
                key_grad = partial[b][1] + key_grad
            held[GK, h, b] = (key_grad * scale).astype(jnp.bfloat16)
            give_back(GK, h, b)

    pl.semaphore_wait(barrier, 3 + sum(jnp.where(exists[side], 1, 0) for side in (UP, DN)))

    for h in range(2):
        loaded(KV, h)
        z_shard(KV, h, mine)
    for t, h in ((KV, 0), (KV, 1), (QG, 0)):
        for mate in mates:
            exchange(mate, t, h)

    pltpu.make_async_copy(mask_hbm, mask_ref, mask_sem).wait()
    index = lax.broadcasted_iota(jnp.int32, (8, 128), 0)
    straight = jnp.zeros((8, 128), jnp.float32)
    mirrored = straight
    for d in range(7):
        straight = jnp.where(index == d, (1.0 - mask_ref[d].astype(jnp.float32)) * BIG, straight)
        mirrored = jnp.where(index == d, (1.0 - mask_ref[MIRROR[d]].astype(jnp.float32)) * BIG, mirrored)
    bias[OWN, mine] = jnp.where(flip == 0, straight, mirrored)
    turned[...] = jnp.where(flip == 0, mirrored, straight)

    for mate in mates:
        bias_copy(mate).start()
    for h in range(2):
        row_pair(mates[0], KV, h).wait_recv()
        z_shard(KV, h, beside)

    def exchange_rest(h, carry):
        @pl.when(h < heads)
        def _():
            for mate in mates:
                exchange(mate, KV, h)
        for mate in mates:
            exchange(mate, QG, h - 1)
        return carry

    lax.fori_loop(2, heads + 1, exchange_rest, 0)

    for side in (UP, DN):
        @pl.when(jnp.logical_not(exists[side]))
        def _(side=side):
            stats[side] = jnp.zeros(stats.shape[1:], jnp.float32)
            bias[side] = jnp.full(bias.shape[1:], BIG, jnp.float32)

    for h in range(2):
        for mate in mates[1:]:
            row_pair(mate, KV, h).wait_recv()
            z_shard(KV, h, mate[1])
    row_arrived(QG, 0)
    z_items(QG, 0, (0, 1, 2, 3))
    for mate in mates:
        bias_arrival(mate).wait_recv()
    column = lax.broadcasted_iota(jnp.int32, (8, 128), 1)
    packed[OWN] = functools.reduce(lambda tile, a: jnp.where(column == a, bias[OWN, a], tile), range(1, ROW), bias[OWN, 0])
    at_sides(lambda side: zbias_copy(side, other[side]).start())

    def step(i, carry):
        @pl.when(jnp.logical_and(i >= 1, i + 1 < heads))
        def _():
            row_arrived(KV, i + 1)
            z_items(KV, i + 1, (0, 1, 2, 3))

        @pl.when(jnp.logical_and(i >= 1, i < heads))
        def _():
            row_arrived(QG, i)

        @pl.when(i < heads)
        def _():
            query_side(i)

        @pl.when(jnp.logical_and(i >= 1, i < heads))
        def _():
            z_items(QG, i, (0, 1, 2, 3))

        @pl.when(i == 1)
        def _():
            at_sides(unpack)

        @pl.when(i >= 1)
        def _():
            drain_early(i - 1)
            key_side(i - 1)

        return carry

    def unpack(side):
        zbias_copy(side, side).wait_recv()
        for a in range(ROW):
            bias[side, a] = jnp.broadcast_to(packed[side][:, a:a + 1], (8, 128))

    def drain_early(h):
        for t in (KV, QG):
            for mate in mates:
                row_pair(mate, t, h).wait_send()

        def sent(side):
            z_whole(side, KV, h).wait_send()
            stat_copy(side, other[side], h).wait_send()

        at_sides(sent)

    lax.fori_loop(0, heads + 1, step, 0)

    for mate in mates:
        bias_copy(mate).wait_send()
    at_sides(lambda side: zbias_copy(side, other[side]).wait_send())

    def drain(h, carry):
        at_sides(lambda side: z_whole(side, QG, h).wait_send())
        blocks = held.at[pl.ds(0, 3), h]
        remote(blocks, blocks, ret_send.at[h], ret_recv.at[0], first + real(2)).wait_send()
        four = held.at[:, h, 0]
        pltpu.make_async_copy(four, four, own_sem.at[h]).wait()
        return carry

    lax.fori_loop(0, heads, drain, 0)

    for _, shard, _ in mates:
        block = held.at[0]
        remote(block, block, ret_send.at[0], ret_recv.at[shard], first + real(shard)).wait_recv()


def copy_out(*refs):
    sems = refs[8]
    copies = [pltpu.make_async_copy(refs[j], refs[4 + j], sems.at[j]) for j in range(4)]
    for copy in copies:
        copy.start()
    for copy in copies:
        copy.wait()


def finish(*arrays):
    return pl.pallas_call(
        copy_out,
        name="finish",
        out_shape=tuple(jax.ShapeDtypeStruct(a.shape, a.dtype) for a in arrays),
        in_specs=[pl.BlockSpec(memory_space=pl.ANY)] * 4,
        out_specs=(pl.BlockSpec(memory_space=pltpu.HBM),) * 4,
        scratch_shapes=[pltpu.SemaphoreType.DMA((4,))],
        compiler_params=pltpu.CompilerParams(vmem_limit_bytes=1 << 20),
    )(*arrays)


def local(seq, query, key, value, grad_out, tile_mask):
    rows, features = query.shape
    heads = features // HEAD // ROW
    pairs = rows * rows * features * 7
    dma = pltpu.SemaphoreType.DMA
    results = pl.pallas_call(
        functools.partial(kernel, seq),
        name="radial",
        out_shape=(jax.ShapeDtypeStruct((rows, features), jnp.bfloat16),) * 4,
        in_specs=[pl.BlockSpec(memory_space=pltpu.HBM)] + [pl.BlockSpec(memory_space=pltpu.HBM)] * 4,
        out_specs=(pl.BlockSpec(memory_space=pl.ANY),) * 4,
        scratch_shapes=[
            pltpu.SMEM((7,), jnp.int32),
            dma(()),
            pltpu.VMEM((3, 2, heads, ROW, 2, rows, HEAD), jnp.bfloat16),
            pltpu.VMEM((4, heads, ROW, rows, HEAD), jnp.bfloat16),
            pltpu.VMEM((3, ROW, 8, 128), jnp.float32),
            pltpu.VMEM((8, 128), jnp.float32),
            pltpu.VMEM((3, 8, 128), jnp.float32),
            pltpu.VMEM((3, heads, 8, 128), jnp.float32),
            dma((2, heads)),
            dma((2, heads, 3)), dma((2, heads, ROW)),
            dma((3, 2, heads)), dma((3, 2, heads, ROW)),
            dma((3,)), dma((ROW,)), dma((3,)), dma((3,)),
            dma((3, heads)), dma((3, heads)),
            dma((heads,)), dma((heads,)), dma((ROW,)),
        ],
        compiler_params=pltpu.CompilerParams(
            collective_id=0, has_side_effects=True, vmem_limit_bytes=32 << 20
        ),
        cost_estimate=pl.CostEstimate(
            flops=16 * pairs, transcendentals=2 * pairs // HEAD, bytes_accessed=16 * rows * features
        ),
    )(*(pltpu.with_memory_space_constraint(a, pltpu.HBM) for a in (tile_mask.reshape(7), query, key, value, grad_out)))
    return tuple(finish(*results))


def solution(mesh):
    spec = P(("grp", "seq"), None)
    return jax.shard_map(
        functools.partial(local, mesh.shape["seq"]),
        mesh=mesh,
        in_specs=(spec,) * 4 + (P("seq", None, None, None),),
        out_specs=(spec,) * 4,
        check_vma=False,
    )
```
